128 devices in a mesh: gx: 8 (over y, core), gy: 4 (over x), gz: 4 (over z).
Axes of the slice: x: 4, y: 4, z: 4, core: 2. Of those that a mesh axis runs over, the one named last changes fastest.
Arguments:
- pressure_source: float32 [128, 256, 1024], P('gx', 'gy', 'gz'), may hold values from -6 to 6
- cell_density: float32 [1024], P('gz'), may hold values from 0.3 to 3
- face_density: float32 [1024], P('gz'), may hold values from 0.3 to 3
Outputs:
- smoothed: float32 [128, 256, 1024], P('gx', 'gy', 'gz')
- coarse_solution: float32 [16, 32, 128], P('gx')
The draws below stay inside these ranges and needn't reach their ends.
All inputs are finite; a program needn't handle non-finite values.
Results may differ from the reference program's by a relative error of at most 0.0001.
Values sent between devices are 32-bit elements; how exact they have to be, the bound alone decides.
A program may use at most 192 MiB of HBM per device.

```python
import math
import jax
import jax.numpy as jnp

LEVELS = 3
SWEEPS = 6
COARSE_SWEEPS = 8
NX = 128
NY = 256
NZ = 1024


def block_scale(own_key, shape, split, smallest, largest):
    loudness = 1.0
    for axis_at, parts in split:
        heights = jax.random.uniform(jax.random.fold_in(jax.random.fold_in(own_key, 6), axis_at), (parts,), jnp.float32, smallest / len(split), largest / len(split))
        loudness = loudness * jnp.repeat(jnp.exp(heights), shape[axis_at] // parts).reshape((-1,) + (1,) * (len(shape) - 1 - axis_at))
    return loudness


def bell_draw(stream_key, shape, scale, limit, shards=(), held_as=jnp.bfloat16):
    result = scale * jax.random.normal(stream_key, shape, jnp.float32)
    if shards:
        result = result * block_scale(stream_key, shape, shards, -0.22, 0.18)
    return jnp.clip(result, -limit, limit).astype(held_as)


def setup_inputs(seed: int = 0) -> dict:
    key_of = jax.random.split(jax.random.key(seed), 4)
    return {
        "pressure_source": bell_draw(key_of[0], (NX, NY, NZ), 1.0, 6.0, ((0, 8), (1, 4), (2, 4)), jnp.float32),
        "cell_density": jnp.clip(jnp.exp(math.log(3.0) - 2.3025851 * jax.random.uniform(key_of[1], (NZ,), jnp.float32) ** block_scale(key_of[1], (NZ,), ((0, 4),), -0.2, 0.2)), 0.3, 3.0),
        "face_density": jnp.clip(jnp.exp(math.log(3.0) - 2.3025851 * jax.random.uniform(key_of[2], (NZ,), jnp.float32) ** block_scale(key_of[2], (NZ,), ((0, 4),), -0.2, 0.2)), 0.3, 3.0),
    }


damping = 0.8


def stencil_apply(iterate, centre_coef, below_coef, above_coef):
    horizontal = 4.0 * iterate - jnp.roll(iterate, 1, 0) - jnp.roll(iterate, -1, 0) - jnp.roll(iterate, 1, 1) - jnp.roll(iterate, -1, 1)
    zero_plane = jnp.zeros_like(iterate[:, :, :1])
    beneath = jnp.concatenate([zero_plane, iterate[:, :, :-1]], axis=2)
    overhead = jnp.concatenate([iterate[:, :, 1:], zero_plane], axis=2)
    return centre_coef * horizontal + below_coef * (iterate - beneath) + above_coef * (iterate - overhead)


def smooth_field(source_term, centre_coef, below_coef, above_coef, sweep_count):
    inverse_diag = 1.0 / (4.0 * centre_coef + below_coef + above_coef)
    iterate = damping * source_term * inverse_diag
    for sweep_index in range(sweep_count - 1):
        iterate = iterate + damping * (source_term - stencil_apply(iterate, centre_coef, below_coef, above_coef)) * inverse_diag
    return iterate


def restrict(residual):
    extent = residual.shape
    blocks = residual.reshape(extent[0] // 2, 2, extent[1] // 2, 2, extent[2] // 2, 2)
    return 0.5 * jnp.sum(blocks, axis=(1, 3, 5))


def reference(pressure_source, cell_density, face_density):
    centre_coef = cell_density
    below_coef = face_density
    above_coef = jnp.concatenate([face_density[1:], jnp.zeros((1,), jnp.float32)])
    source_term = pressure_source
    smoothed = pressure_source
    for level_index in range(LEVELS):
        iterate = smooth_field(source_term, centre_coef, below_coef, above_coef, SWEEPS)
        if level_index == 0:
            smoothed = iterate
        residual = source_term - stencil_apply(iterate, centre_coef, below_coef, above_coef)
        source_term = restrict(residual)
        centre_coef = 0.5 * (centre_coef[0::2] + centre_coef[1::2])
        below_coef = below_coef[0::2]
        above_coef = above_coef[1::2]
    coarse_solution = smooth_field(source_term, centre_coef, below_coef, above_coef, COARSE_SWEEPS)
    return smoothed, coarse_solution
```

```python
import jax
import jax.numpy as jnp
from jax import lax
from jax.experimental import pallas as pl
from jax.experimental.pallas import tpu as pltpu
from jax.sharding import PartitionSpec as P

MESH = pl.DeviceIdType.MESH
AXES = ("gx", "gy", "gz")
COUNTS = (8, 4, 4)
SWEEPS = 6
COARSE_SWEEPS = 8
HALO = 6
XO = 8
YO = 16
LANES = 128
DAMPING = 0.8

LEVELS = (
    dict(x=16, y=64, own=2, tiles=3, block=8, reach=1, shape=(3, 3, 32, 96, LANES)),
    dict(x=8, y=32, own=1, tiles=2, block=8, reach=1, shape=(3, 2, 24, 64, LANES)),
    dict(x=4, y=16, own=1, tiles=1, block=4, reach=2, shape=(3, 1, 20, 48, LANES)),
)


def coordinates():
    return tuple(lax.axis_index(a) for a in AXES)


def device_at(place, offset):
    return tuple(
        lax.rem(p + (o + n), n) if o else p for p, o, n in zip(place, offset, COUNTS)
    )


def offsets_of(level):
    reach = level["reach"]
    return [
        (dx, dy, dz)
        for dx in range(-reach, reach + 1)
        for dy in (-1, 0, 1)
        for dz in (-1, 0, 1)
        if (dx, dy, dz) != (0, 0, 0)
    ]


FACES = ((1, 0, 0), (-1, 0, 0), (0, 1, 0), (0, -1, 0), (0, 0, 1), (0, 0, -1))
PROFILE_PEERS = ((0, 0, 1), (0, 0, -1), (0, 0, 2))
COLUMN_PEERS = tuple(
    (dx, dy, 0) for dx in (4, 3, -3, 2, -2, 1, -1, 0) for dy in (2, 1, -1, 0) if (dx, dy) != (0, 0)
)


def lane_iota(rows=8):
    return lax.broadcasted_iota(jnp.int32, (rows, LANES), 1)


def select_dot(rows, picks):
    return jnp.dot(
        rows, picks, preferred_element_type=jnp.float32, precision=lax.Precision.HIGHEST
    )


def halving(shift, value, parity=None):
    k = lax.broadcasted_iota(jnp.int32, (LANES, LANES), 0)
    l = 2 * (lax.broadcasted_iota(jnp.int32, (LANES, LANES), 1) - shift)
    if parity is None:
        hit = (k == l) | (k == l + 1)
    else:
        hit = k == l + parity
    return jnp.where(hit, jnp.float32(value), jnp.float32(0.0))


def message(level, raw, packed, ext, received, offset):
    dx, dy, dz = offset
    nx, ny, own = level["x"], level["y"], level["own"]
    if dz == 0:
        if dx == 0:
            sx, tx, width = 0, XO, nx
        elif dx > 0:
            width = min(nx, HALO - (dx - 1) * nx)
            sx, tx = nx - width, XO - (dx - 1) * nx - width
        else:
            width = min(nx, HALO - (-dx - 1) * nx)
            sx, tx = 0, XO + nx + (-dx - 1) * nx
        if dy == 0:
            sy, ty, rows = 0, YO, ny
        elif dy > 0:
            sy, ty, rows = ny - 8, YO - 8, 8
        else:
            sy, ty, rows = 0, YO + ny, 8
        return (
            raw.at[pl.ds(0, own), pl.ds(sx, width), pl.ds(sy, rows), :],
            ext.at[0, pl.ds(0, own), pl.ds(tx, width), pl.ds(ty, rows), :],
        )
    blocks, strips, reach = nx // level["block"], ny // 8, level["reach"]
    if dx == 0:
        sb, tb, nb = 0, reach, blocks
    elif dx > 0:
        sb, tb, nb = blocks - 1, reach - dx, 1
    else:
        sb, tb, nb = 0, reach + blocks - 1 - dx, 1
    if dy == 0:
        ss, ts, ns = 0, 1, strips
    elif dy > 0:
        ss, ts, ns = strips - 1, 0, 1
    else:
        ss, ts, ns = 0, strips + 1, 1
    return (
        packed.at[pl.ds(sb, nb), pl.ds(ss, ns), :, :],
        received.at[0 if dz > 0 else 1, pl.ds(tb, nb), pl.ds(ts, ns), :, :],
    )


def pack_faces(level, raw, packed):
    lane = lane_iota()
    group = lane // 8
    own, block, strips = level["own"], level["block"], level["y"] // 8
    far = 15 if level["tiles"] > 1 else 7

    def strip(s, carry):
        rows = pl.ds(pl.multiple_of(8 * s, 8), 8)
        for b in range(level["x"] // block):
            total = jnp.zeros((8, LANES), jnp.float32)
            for i in range(block):
                ends = raw[0, b * block + i, rows, :]
                if own == 2:
                    ends = jnp.where(lane < 64, ends, raw[1, b * block + i, rows, :])
                moved = pltpu.roll(ends, 16 * i, 1) if i else ends
                mine = (group == 2 * i) | (group == (2 * i + far) % 16)
                total = jnp.where(mine, moved, total)
            packed[b, s] = total
        return carry

    lax.fori_loop(0, strips, strip, 0)


def stencil(level_tiles, wanted, ext, slot, x, row, coefs):
    lane = lane_iota()
    centre = [ext[slot, t, x, pl.ds(row, 8), :] for t in range(level_tiles)]
    up = [pltpu.roll(v, 1, 1) for v in centre]
    down = [pltpu.roll(v, LANES - 1, 1) for v in centre]
    sums = []
    for t in range(wanted):
        beneath, overhead = up[t], down[t]
        if level_tiles > 1:
            beneath = jnp.where(lane == 0, up[t - 1], beneath)
            overhead = jnp.where(lane == LANES - 1, down[(t + 1) % level_tiles], overhead)
        around = (
            ext[slot, t, x - 1, pl.ds(row, 8), :] + ext[slot, t, x + 1, pl.ds(row, 8), :]
        ) + (ext[slot, t, x, pl.ds(row - 1, 8), :] + ext[slot, t, x, pl.ds(row + 1, 8), :])
        c, low, high, _, _ = coefs[t]
        sums.append(c * around + (low * beneath + high * overhead))
    return centre, sums


def sweep_slots(s):
    source = jnp.where(s == 1, 0, 1 + lax.rem(s, 2))
    return source, 1 + lax.rem(s + 1, 2)


def relax(level, ext, coefs):
    tiles, nx, strips = level["tiles"], level["x"], level["y"] // 8 + 2

    def sweep(s, carry):
        source, target = sweep_slots(s)

        def plane(x, inner):
            for j in range(strips):
                row = 8 + 8 * j
                centre, sums = stencil(tiles, tiles, ext, source, x, row, coefs)
                for t in range(tiles):
                    beta = ext[0, t, x, pl.ds(row, 8), :]
                    ext[target, t, x, pl.ds(row, 8), :] = (0.2 * centre[t] + beta) + sums[t]
            return inner

        lax.fori_loop(XO - HALO + s, XO + nx + HALO - s, plane, 0)
        return carry

    lax.fori_loop(1, SWEEPS, sweep, 0)


def begin(level, raw, received, ext, coefs):
    tiles, own, nx, block = level["tiles"], level["own"], level["x"], level["block"]
    strips = level["y"] // 8 + 2
    lane = lane_iota()
    even = lax.rem(lane // 8, 2) == 0
    base = 64 if tiles == 1 else 0

    def halo_tile(x, j):
        e, i = x // block, lax.rem(x, block)
        both = jnp.where(even, received[1, e, j], received[0, e, j])
        return pltpu.roll(both, lax.rem(base + LANES - 16 * i, LANES), 1)

    def plane_of(inside):
        def plane(x, carry):
            for j in range(strips):
                row = 8 + 8 * j
                ends = halo_tile(x, j)
                for t in range(own):
                    if inside and 0 < j < strips - 1:
                        b = raw[t, x - XO, pl.ds(8 * (j - 1), 8), :]
                    else:
                        b = ext[0, t, x, pl.ds(row, 8), :]
                    if tiles == 1:
                        b = jnp.where(lane < 64, b, ends)
                    ext[0, t, x, pl.ds(row, 8), :] = b * coefs[t][3]
                if tiles > 1:
                    ext[0, own, x, pl.ds(row, 8), :] = ends * coefs[own][3]
            return carry

        return plane

    lax.fori_loop(XO - HALO, XO, plane_of(False), 0)
    lax.fori_loop(XO, XO + nx, plane_of(True), 0)
    lax.fori_loop(XO + nx, XO + nx + HALO, plane_of(False), 0)


def residual_rows(level, ext, coefs, pair, halved):
    tiles, own, nx, ny = level["tiles"], level["own"], level["x"], level["y"]
    slot = 1

    def planes(p, carry):
        for j in range(ny // 8):
            row = YO + 8 * j
            total = [None] * own
            for k in range(2):
                x = XO + 2 * p + k
                centre, sums = stencil(tiles, own, ext, slot, x, row, coefs)
                for t in range(own):
                    beta = ext[0, t, x, pl.ds(row, 8), :]
                    r = (beta - 0.8 * centre[t]) + sums[t]
                    total[t] = r if k == 0 else total[t] + r
            for t in range(own):
                pair[t, pl.ds(8 * j, 8), :] = total[t] * coefs[t][4]
        for t in range(own):
            halved[t, p] = (
                pair[t, pl.ds(0, ny // 2, stride=2), :] + pair[t, pl.ds(1, ny // 2, stride=2), :]
            )
        return carry

    lax.fori_loop(0, nx // 2, planes, 0)


def kernel(
    source_ref,
    cell_ref,
    face_ref,
    smooth_ref,
    coarse_ref,
    raw0,
    raw1,
    raw2,
    ext0,
    ext1,
    ext2,
    ext3,
    packed0,
    packed1,
    packed2,
    received0,
    received1,
    received2,
    profile,
    tables,
    spread,
    constants,
    pair,
    halved0,
    halved1,
    halved2,
    column,
    slab,
    send,
    recv,
    local,
    greet,
):
    place = coordinates()
    gx, gy, gz = place
    counter = [0]

    def remote(source, target, offset):
        k = counter[0]
        counter[0] += 1
        return pltpu.make_async_remote_copy(
            src_ref=source,
            dst_ref=target,
            send_sem=send.at[k],
            recv_sem=recv.at[k],
            device_id=device_at(place, offset),
            device_id_type=MESH,
        )

    raws, exts = (raw0, raw1, raw2), (ext0, ext1, ext2)
    packs, receiveds = (packed0, packed1, packed2), (received0, received1, received2)
    halveds = (halved0, halved1, halved2)

    barrier = pltpu.get_barrier_semaphore()
    peers = FACES + ((0, 0, 2),)
    for offset in peers:
        pl.semaphore_signal(
            barrier, inc=1, device_id=device_at(place, offset), device_id_type=MESH
        )
    loads = [
        pltpu.make_async_copy(
            source_ref.at[:, :, pl.ds(LANES * t, LANES)], raw0.at[t], local.at[t]
        )
        for t in range(2)
    ]
    for c in loads:
        c.start()
    mine = profile.at[gz]
    for t in range(2):
        profile[gz, pl.ds(t, 1), :] = cell_ref[pl.ds(LANES * t, LANES)].reshape(1, LANES)
        profile[gz, pl.ds(2 + t, 1), :] = face_ref[pl.ds(LANES * t, LANES)].reshape(1, LANES)
    for c in loads:
        c.wait()
    pack_faces(LEVELS[0], raw0, packed0)
    pl.semaphore_wait(barrier, len(peers))

    pending = []
    copies = {}
    for offset in offsets_of(LEVELS[0]):
        copies[offset] = remote(
            *message(LEVELS[0], raw0, packed0, ext0, received0, offset), offset
        )
    profiles = [remote(mine, mine, offset) for offset in PROFILE_PEERS]
    for offset in FACES:
        copies[offset].start()
    for c in profiles:
        c.start()
    for stage, distance in ((0, 2), (1, 3)):
        for offset in FACES:
            pl.semaphore_signal(
                greet.at[stage], inc=1, device_id=device_at(place, offset), device_id_type=MESH
            )
        pl.semaphore_wait(greet.at[stage], len(FACES))
        for offset in copies:
            if sum(abs(o) for o in offset) == distance:
                copies[offset].start()
    pending += list(copies.values()) + profiles

    for c in profiles:
        c.wait_recv()
    lane = lane_iota()
    row = lax.broadcasted_iota(jnp.int32, (8, LANES), 0)
    for z in range(4):
        for t in range(2):
            tables[0, pl.ds(2 * z + t, 1), :] = profile[z, pl.ds(t, 1), :]
            tables[1, pl.ds(2 * z + t, 1), :] = profile[z, pl.ds(2 + t, 1), :]
    cell, below = tables[0], tables[1]
    turned = pltpu.roll(below, LANES - 1, 1)
    above = jnp.where(lane == LANES - 1, pltpu.roll(turned, 7, 0), turned)
    above = jnp.where((row == 7) & (lane == LANES - 1), 0.0, above)
    first, second = halving(0, 1.0, 0), halving(0, 1.0, 1)
    first, second = first + halving(64, 1.0, 0), second + halving(64, 1.0, 1)
    for n in range(4):
        scale = DAMPING / (4.0 * cell + below + above)
        constants[n, 0] = cell * scale
        constants[n, 1] = jnp.where((row == 0) & (lane == 0), 0.0, below * scale)
        constants[n, 2] = above * scale
        constants[n, 3] = scale
        constants[n, 4] = (4.0 * cell + below + above) * (1.0 / DAMPING)
        if n < 3:
            spread[0, pl.ds(0, 8), :] = 0.5 * (select_dot(cell, first) + select_dot(cell, second))
            spread[1, pl.ds(0, 8), :] = select_dot(below, first)
            spread[2, pl.ds(0, 8), :] = select_dot(above, second)
            narrow = [
                jnp.where(
                    lane < 64,
                    spread[k, pl.ds(0, 8, stride=2), :],
                    spread[k, pl.ds(1, 8, stride=2), :],
                )
                for k in range(3)
            ]
            used = row < 8 >> (n + 1)
            cell, below = jnp.where(used, narrow[0], 1.0), jnp.where(used, narrow[1], 1.0)
            above = jnp.where(used, narrow[2], 1.0)

    def row_of(n, k, r):
        return jnp.broadcast_to(constants[n, k, pl.ds(r, 1), :], (8, LANES))

    def level_coefs(n):
        if n == 0:
            tiles = [lambda k, t=t: row_of(0, k, 2 * gz + t) for t in range(2)]
            tiles.append(
                lambda k: jnp.where(
                    lane < 64,
                    row_of(0, k, lax.rem(2 * gz + 2, 8)),
                    row_of(0, k, lax.rem(2 * gz + 7, 8)),
                )
            )
        elif n == 1:
            tiles = [
                lambda k: row_of(1, k, gz),
                lambda k: jnp.where(
                    lane < 64,
                    row_of(1, k, lax.rem(gz + 1, 4)),
                    row_of(1, k, lax.rem(gz + 3, 4)),
                ),
            ]
        elif n == 2:

            def one(k):
                here, there = row_of(2, k, gz // 2), row_of(2, k, 1 - gz // 2)
                lower = jnp.where(lane < 96, here, there)
                upper = pltpu.roll(jnp.where(lane < 32, there, here), 64, 1)
                return jnp.where(lax.rem(gz, 2) == 0, lower, upper)

            tiles = [one]
        else:
            tiles = [lambda k: row_of(3, k, 0)]
        return [[tile(k) for k in range(5)] for tile in tiles]

    for n, level in enumerate(LEVELS):
        raw, ext, packed, received, halved = raws[n], exts[n], packs[n], receiveds[n], halveds[n]
        if n > 0:
            pack_faces(level, raw, packed)
            copies = {}
            order = sorted(offsets_of(level), key=lambda o: -sum(abs(i) for i in o))
            for offset in order:
                copies[offset] = remote(
                    *message(level, raw, packed, ext, received, offset), offset
                )
                copies[offset].start()
            pending += list(copies.values())
        coefs = level_coefs(n)
        for c in copies.values():
            c.wait_recv()
        begin(level, raw, received, ext, coefs)
        relax(level, ext, coefs)
        if n == 0:
            stores = [
                pltpu.make_async_copy(
                    ext0.at[1, t, pl.ds(XO, 16), pl.ds(YO, 64), :],
                    smooth_ref.at[:, :, pl.ds(LANES * t, LANES)],
                    local.at[2 + t],
                )
                for t in range(2)
            ]
            for c in stores:
                c.start()
        residual_rows(level, ext, coefs, pair, halved)
        if n == 0:
            total = select_dot(halved[0].reshape(256, LANES), halving(0, 0.5)) + select_dot(
                halved[1].reshape(256, LANES), halving(64, 0.5)
            )
            raw1[0] = total.reshape(8, 32, LANES)
        elif n == 1:
            raw2[0] = select_dot(halved[0].reshape(64, LANES), halving(0, 0.5)).reshape(
                4, 16, LANES
            )
        else:
            k = lax.broadcasted_iota(jnp.int32, (LANES, LANES), 0)
            picks = jnp.where(k < 64, halving(32 * gz, 0.5), 0.0)
            column[gz] = select_dot(halved[0].reshape(16, LANES), picks).reshape(2, 8, LANES)

    copies = [remote(column.at[gz], column.at[gz], offset) for offset in PROFILE_PEERS]
    for c in copies:
        c.start()
    pending += copies
    coefs = level_coefs(3)
    for c in copies:
        c.wait_recv()
    whole = (column[0] + column[1]) + (column[2] + column[3])
    slab[...] = whole
    strip = pl.ds(pl.multiple_of(8 + 8 * gy, 8), 8)
    copies = [
        remote(slab, ext3.at[0, 0, pl.ds(8 - 2 * offset[0], 2), strip, :], offset)
        for offset in COLUMN_PEERS
    ]
    for c in copies:
        c.start()
    ext3[0, 0, pl.ds(8, 2), strip, :] = whole
    for c in pending:
        c.wait_send()
    for c in copies:
        c.wait_recv()

    def wrapped(slot, x, values):
        for j in range(6):
            ext3[slot, 0, x, pl.ds(8 * j, 8), :] = values[(j - 1) % 4]

    ext3[0, 0, 16] = ext3[0, 0, 0]

    def start_all(x, carry):
        wrapped(0, x, [ext3[0, 0, x, pl.ds(8 + 8 * j, 8), :] * coefs[0][3] for j in range(4)])
        return carry

    lax.fori_loop(1, 17, start_all, 0)

    def coarse_sweep(s, carry):
        source, target = sweep_slots(s)

        def plane(x, inner):
            values = []
            for j in range(4):
                r = 8 + 8 * j
                centre, sums = stencil(1, 1, ext3, source, x, r, coefs)
                beta = ext3[0, 0, x, pl.ds(r, 8), :]
                values.append((0.2 * centre[0] + beta) + sums[0])
            wrapped(target, x, values)
            return inner

        lax.fori_loop(1 + s, 17 - s, plane, 0)
        return carry

    lax.fori_loop(1, COARSE_SWEEPS, coarse_sweep, 0)
    coarse_ref[...] = ext3[1, 0, pl.ds(8, 2), pl.ds(8, 32), :]
    for c in copies:
        c.wait_send()
    for c in stores:
        c.wait()


def on_device(source, cell, face):
    f32 = jnp.float32
    messages = sum(len(offsets_of(level)) for level in LEVELS) + 6 + len(COLUMN_PEERS)
    vmem = pl.BlockSpec(memory_space=pltpu.VMEM)
    hbm = pl.BlockSpec(memory_space=pl.ANY)
    tile = (8, LANES)
    return pl.pallas_call(
        kernel,
        out_shape=(
            jax.ShapeDtypeStruct((16, 64, 256), f32),
            jax.ShapeDtypeStruct((2, 32, 128), f32),
        ),
        in_specs=[hbm, vmem, vmem],
        out_specs=(hbm, vmem),
        scratch_shapes=[
            pltpu.VMEM((2, 16, 64, LANES), f32),
            pltpu.VMEM((1, 8, 32, LANES), f32),
            pltpu.VMEM((1, 4, 16, LANES), f32),
            pltpu.VMEM(LEVELS[0]["shape"], f32),
            pltpu.VMEM(LEVELS[1]["shape"], f32),
            pltpu.VMEM(LEVELS[2]["shape"], f32),
            pltpu.VMEM((3, 1, 18, 48, LANES), f32),
            pltpu.VMEM((2, 8) + tile, f32),
            pltpu.VMEM((1, 4) + tile, f32),
            pltpu.VMEM((1, 2) + tile, f32),
            pltpu.VMEM((2, 4, 10) + tile, f32),
            pltpu.VMEM((2, 3, 6) + tile, f32),
            pltpu.VMEM((2, 5, 4) + tile, f32),
            pltpu.VMEM((4,) + tile, f32),
            pltpu.VMEM((2,) + tile, f32),
            pltpu.VMEM((3, 16, LANES), f32),
            pltpu.VMEM((4, 5) + tile, f32),
            pltpu.VMEM((2, 64, LANES), f32),
            pltpu.VMEM((2, 8, 32, LANES), f32),
            pltpu.VMEM((1, 4, 16, LANES), f32),
            pltpu.VMEM((1, 2, 8, LANES), f32),
            pltpu.VMEM((4, 2) + tile, f32),
            pltpu.VMEM((2,) + tile, f32),
            pltpu.SemaphoreType.DMA((messages,)),
            pltpu.SemaphoreType.DMA((messages,)),
            pltpu.SemaphoreType.DMA((4,)),
            pltpu.SemaphoreType.REGULAR((2,)),
        ],
        compiler_params=pltpu.CompilerParams(
            collective_id=0, has_side_effects=True, vmem_limit_bytes=48 << 20
        ),
    )(source, cell, face)


def solution(mesh):
    return jax.shard_map(
        on_device,
        mesh=mesh,
        in_specs=(P("gx", "gy", "gz"), P("gz"), P("gz")),
        out_specs=(P("gx", "gy", "gz"), P("gx", None, None)),
        check_vma=False,
    )
```

```python
import jax
import jax.numpy as jnp
from jax import lax
from jax.experimental import pallas as pl
from jax.experimental.pallas import tpu as pltpu
from jax.sharding import PartitionSpec as P

MESH = pl.DeviceIdType.MESH
AXES = ("gx", "gy", "gz")
COUNTS = (8, 4, 4)
SWEEPS = 6
COARSE_SWEEPS = 8
HALO = 6
XO = 8
YO = 16
LANES = 128
DAMPING = 0.8

LEVELS = (
    dict(x=16, y=64, own=2, tiles=3, block=8, reach=1, shape=(3, 32, 96, LANES)),
    dict(x=8, y=32, own=1, tiles=2, block=8, reach=1, shape=(2, 24, 64, LANES)),
    dict(x=4, y=16, own=1, tiles=1, block=4, reach=2, shape=(1, 20, 48, LANES)),
)


def coordinates():
    return tuple(lax.axis_index(a) for a in AXES)


def device_at(place, offset):
    return tuple(
        lax.rem(p + (o + n), n) if o else p for p, o, n in zip(place, offset, COUNTS)
    )


def offsets_of(level):
    reach = level["reach"]
    return [
        (dx, dy, dz)
        for dx in range(-reach, reach + 1)
        for dy in (-1, 0, 1)
        for dz in (-1, 0, 1)
        if (dx, dy, dz) != (0, 0, 0)
    ]


FACES = ((1, 0, 0), (-1, 0, 0), (0, 1, 0), (0, -1, 0), (0, 0, 1), (0, 0, -1))
PROFILE_PEERS = ((0, 0, 1), (0, 0, -1), (0, 0, 2))
COLUMN_PEERS = tuple(
    (dx, dy, 0) for dx in (4, 3, -3, 2, -2, 1, -1, 0) for dy in (2, 1, -1, 0) if (dx, dy) != (0, 0)
)


def lane_iota(rows=8):
    return lax.broadcasted_iota(jnp.int32, (rows, LANES), 1)


def select_dot(rows, picks):
    return jnp.dot(
        rows, picks, preferred_element_type=jnp.float32, precision=lax.Precision.HIGHEST
    )


def halving(shift, value, parity=None):
    k = lax.broadcasted_iota(jnp.int32, (LANES, LANES), 0)
    l = 2 * (lax.broadcasted_iota(jnp.int32, (LANES, LANES), 1) - shift)
    if parity is None:
        hit = (k == l) | (k == l + 1)
    else:
        hit = k == l + parity
    return jnp.where(hit, jnp.float32(value), jnp.float32(0.0))


def message(level, raw, packed, ext, received, offset):
    dx, dy, dz = offset
    nx, ny, own = level["x"], level["y"], level["own"]
    if dz == 0:
        if dx == 0:
            sx, tx, width = 0, XO, nx
        elif dx > 0:
            width = min(nx, HALO - (dx - 1) * nx)
            sx, tx = nx - width, XO - (dx - 1) * nx - width
        else:
            width = min(nx, HALO - (-dx - 1) * nx)
            sx, tx = 0, XO + nx + (-dx - 1) * nx
        if dy == 0:
            sy, ty, rows = 0, YO, ny
        elif dy > 0:
            sy, ty, rows = ny - 8, YO - 8, 8
        else:
            sy, ty, rows = 0, YO + ny, 8
        return (
            raw.at[pl.ds(0, own), pl.ds(sx, width), pl.ds(sy, rows), :],
            ext.at[pl.ds(0, own), pl.ds(tx, width), pl.ds(ty, rows), :],
        )
    blocks, strips, reach = nx // level["block"], ny // 8, level["reach"]
    if dx == 0:
        sb, tb, nb = 0, reach, blocks
    elif dx > 0:
        sb, tb, nb = blocks - 1, reach - dx, 1
    else:
        sb, tb, nb = 0, reach + blocks - 1 - dx, 1
    if dy == 0:
        ss, ts, ns = 0, 1, strips
    elif dy > 0:
        ss, ts, ns = strips - 1, 0, 1
    else:
        ss, ts, ns = 0, strips + 1, 1
    return (
        packed.at[pl.ds(sb, nb), pl.ds(ss, ns), :, :],
        received.at[0 if dz > 0 else 1, pl.ds(tb, nb), pl.ds(ts, ns), :, :],
    )


def pack_faces(level, raw, packed):
    lane = lane_iota()
    group = lane // 8
    own, block, strips = level["own"], level["block"], level["y"] // 8
    far = 15 if level["tiles"] > 1 else 7

    def strip(s, carry):
        rows = pl.ds(pl.multiple_of(8 * s, 8), 8)
        for b in range(level["x"] // block):
            total = jnp.zeros((8, LANES), jnp.float32)
            for i in range(block):
                ends = raw[0, b * block + i, rows, :]
                if own == 2:
                    ends = jnp.where(lane < 64, ends, raw[1, b * block + i, rows, :])
                moved = pltpu.roll(ends, 16 * i, 1) if i else ends
                mine = (group == 2 * i) | (group == (2 * i + far) % 16)
                total = jnp.where(mine, moved, total)
            packed[b, s] = total
        return carry

    lax.fori_loop(0, strips, strip, 0)


def stencil(level_tiles, wanted, ext, x, row, coefs):
    lane = lane_iota()
    centre = [ext[t, x, pl.ds(row, 8), :] for t in range(level_tiles)]
    up = [pltpu.roll(v, 1, 1) for v in centre]
    down = [pltpu.roll(v, LANES - 1, 1) for v in centre]
    sums = []
    for t in range(wanted):
        beneath, overhead = up[t], down[t]
        if level_tiles > 1:
            beneath = jnp.where(lane == 0, up[t - 1], beneath)
            overhead = jnp.where(lane == LANES - 1, down[(t + 1) % level_tiles], overhead)
        around = (
            ext[t, x - 1, pl.ds(row, 8), :] + ext[t, x + 1, pl.ds(row, 8), :]
        ) + (ext[t, x, pl.ds(row - 1, 8), :] + ext[t, x, pl.ds(row + 1, 8), :])
        c, low, high, _, _ = coefs[t]
        sums.append(c * around + (low * beneath + high * overhead))
    return centre, sums


def update(tiles, beta, source, target, first, last, strips, coefs, finish):
    def plane(x, carry):
        values = []
        for j in range(strips):
            row = 8 + 8 * j
            centre, sums = stencil(tiles, tiles, source, x, row, coefs)
            for t in range(tiles):
                if source is beta:
                    values.append(1.2 * centre[t] + sums[t])
                else:
                    values.append((0.2 * centre[t] + beta[t, x, pl.ds(row, 8), :]) + sums[t])
        finish(target, x, values)
        return carry

    lax.fori_loop(first, last, plane, 0)


def sweeps(tiles, beta, ping, pong, first, last, count, strips, coefs, finish):
    update(tiles, beta, beta, ping, first + 1, last - 1, strips, coefs, finish)

    def two(k, carry):
        s = 2 * k + 2
        update(tiles, beta, ping, pong, first + s, last - s, strips, coefs, finish)
        update(tiles, beta, pong, ping, first + s + 1, last - s - 1, strips, coefs, finish)
        return carry

    lax.fori_loop(0, (count - 1) // 2, two, 0)


def relax(level, ext, ping, pong, coefs):
    tiles, nx, strips = level["tiles"], level["x"], level["y"] // 8 + 2

    def finish(target, x, values):
        for j in range(strips):
            for t in range(tiles):
                target[t, x, pl.ds(8 + 8 * j, 8), :] = values[j * tiles + t]

    sweeps(
        tiles, ext, ping, pong, XO - HALO, XO + nx + HALO, SWEEPS - 1, strips, coefs, finish
    )


def begin(level, raw, received, ext, coefs):
    tiles, own, nx, block = level["tiles"], level["own"], level["x"], level["block"]
    strips = level["y"] // 8 + 2
    lane = lane_iota()
    even = lax.rem(lane // 8, 2) == 0
    base = 64 if tiles == 1 else 0

    def halo_tile(x, j):
        e, i = x // block, lax.rem(x, block)
        both = jnp.where(even, received[1, e, j], received[0, e, j])
        return pltpu.roll(both, lax.rem(base + LANES - 16 * i, LANES), 1)

    def plane_of(inside):
        def plane(x, carry):
            for j in range(strips):
                row = 8 + 8 * j
                ends = halo_tile(x, j)
                for t in range(own):
                    if inside and 0 < j < strips - 1:
                        b = raw[t, x - XO, pl.ds(8 * (j - 1), 8), :]
                    else:
                        b = ext[t, x, pl.ds(row, 8), :]
                    if tiles == 1:
                        b = jnp.where(lane < 64, b, ends)
                    ext[t, x, pl.ds(row, 8), :] = b * coefs[t][3]
                if tiles > 1:
                    ext[own, x, pl.ds(row, 8), :] = ends * coefs[own][3]
            return carry

        return plane

    lax.fori_loop(XO - HALO, XO, plane_of(False), 0)
    lax.fori_loop(XO, XO + nx, plane_of(True), 0)
    lax.fori_loop(XO + nx, XO + nx + HALO, plane_of(False), 0)


def residual_rows(level, ext, ping, coefs, pair, halved):
    tiles, own, nx, ny = level["tiles"], level["own"], level["x"], level["y"]

    def planes(p, carry):
        for j in range(ny // 8):
            row = YO + 8 * j
            total = [None] * own
            for k in range(2):
                x = XO + 2 * p + k
                centre, sums = stencil(tiles, own, ping, x, row, coefs)
                for t in range(own):
                    beta = ext[t, x, pl.ds(row, 8), :]
                    r = (beta - 0.8 * centre[t]) + sums[t]
                    total[t] = r if k == 0 else total[t] + r
            for t in range(own):
                pair[t, pl.ds(8 * j, 8), :] = total[t] * coefs[t][4]
        for t in range(own):
            halved[t, p] = (
                pair[t, pl.ds(0, ny // 2, stride=2), :] + pair[t, pl.ds(1, ny // 2, stride=2), :]
            )
        return carry

    lax.fori_loop(0, nx // 2, planes, 0)


def kernel(
    source_ref,
    cell_ref,
    face_ref,
    smooth_ref,
    coarse_ref,
    raw0,
    raw1,
    raw2,
    ext0,
    ext1,
    ext2,
    ext3,
    ping0,
    ping1,
    ping2,
    ping3,
    pong0,
    pong1,
    pong2,
    pong3,
    packed0,
    packed1,
    packed2,
    received0,
    received1,
    received2,
    profile,
    tables,
    spread,
    constants,
    pair,
    halved0,
    halved1,
    halved2,
    column,
    slab,
    send,
    recv,
    local,
    greet,
):
    place = coordinates()
    gx, gy, gz = place
    counter = [0]

    def remote(source, target, offset):
        k = counter[0]
        counter[0] += 1
        return pltpu.make_async_remote_copy(
            src_ref=source,
            dst_ref=target,
            send_sem=send.at[k],
            recv_sem=recv.at[k],
            device_id=device_at(place, offset),
            device_id_type=MESH,
        )

    pings, pongs = (ping0, ping1, ping2), (pong0, pong1, pong2)
    raws, exts = (raw0, raw1, raw2), (ext0, ext1, ext2)
    packs, receiveds = (packed0, packed1, packed2), (received0, received1, received2)
    halveds = (halved0, halved1, halved2)

    barrier = pltpu.get_barrier_semaphore()
    peers = FACES + ((0, 0, 2),)
    for offset in peers:
        pl.semaphore_signal(
            barrier, inc=1, device_id=device_at(place, offset), device_id_type=MESH
        )
    loads = [
        pltpu.make_async_copy(
            source_ref.at[:, :, pl.ds(LANES * t, LANES)], raw0.at[t], local.at[t]
        )
        for t in range(2)
    ]
    for c in loads:
        c.start()
    mine = profile.at[gz]
    for t in range(2):
        profile[gz, pl.ds(t, 1), :] = cell_ref[pl.ds(LANES * t, LANES)].reshape(1, LANES)
        profile[gz, pl.ds(2 + t, 1), :] = face_ref[pl.ds(LANES * t, LANES)].reshape(1, LANES)
    for c in loads:
        c.wait()
    pack_faces(LEVELS[0], raw0, packed0)
    pl.semaphore_wait(barrier, len(peers))

    pending = []
    copies = {}
    for offset in offsets_of(LEVELS[0]):
        copies[offset] = remote(
            *message(LEVELS[0], raw0, packed0, ext0, received0, offset), offset
        )
    profiles = [remote(mine, mine, offset) for offset in PROFILE_PEERS]
    for offset in FACES:
        copies[offset].start()
    for c in profiles:
        c.start()
    for stage, distance in ((0, 2), (1, 3)):
        for offset in FACES:
            pl.semaphore_signal(
                greet.at[stage], inc=1, device_id=device_at(place, offset), device_id_type=MESH
            )
        pl.semaphore_wait(greet.at[stage], len(FACES))
        for offset in copies:
            if sum(abs(o) for o in offset) == distance:
                copies[offset].start()
    pending += list(copies.values()) + profiles

    for c in profiles:
        c.wait_recv()
    lane = lane_iota()
    row = lax.broadcasted_iota(jnp.int32, (8, LANES), 0)
    for z in range(4):
        for t in range(2):
            tables[0, pl.ds(2 * z + t, 1), :] = profile[z, pl.ds(t, 1), :]
            tables[1, pl.ds(2 * z + t, 1), :] = profile[z, pl.ds(2 + t, 1), :]
    cell, below = tables[0], tables[1]
    turned = pltpu.roll(below, LANES - 1, 1)
    above = jnp.where(lane == LANES - 1, pltpu.roll(turned, 7, 0), turned)
    above = jnp.where((row == 7) & (lane == LANES - 1), 0.0, above)
    first, second = halving(0, 1.0, 0), halving(0, 1.0, 1)
    first, second = first + halving(64, 1.0, 0), second + halving(64, 1.0, 1)
    for n in range(4):
        scale = DAMPING / (4.0 * cell + below + above)
        constants[n, 0] = cell * scale
        constants[n, 1] = jnp.where((row == 0) & (lane == 0), 0.0, below * scale)
        constants[n, 2] = above * scale
        constants[n, 3] = scale
        constants[n, 4] = (4.0 * cell + below + above) * (1.0 / DAMPING)
        if n < 3:
            spread[0, pl.ds(0, 8), :] = 0.5 * (select_dot(cell, first) + select_dot(cell, second))
            spread[1, pl.ds(0, 8), :] = select_dot(below, first)
            spread[2, pl.ds(0, 8), :] = select_dot(above, second)
            narrow = [
                jnp.where(
                    lane < 64,
                    spread[k, pl.ds(0, 8, stride=2), :],
                    spread[k, pl.ds(1, 8, stride=2), :],
                )
                for k in range(3)
            ]
            used = row < 8 >> (n + 1)
            cell, below = jnp.where(used, narrow[0], 1.0), jnp.where(used, narrow[1], 1.0)
            above = jnp.where(used, narrow[2], 1.0)

    def row_of(n, k, r):
        return jnp.broadcast_to(constants[n, k, pl.ds(r, 1), :], (8, LANES))

    def level_coefs(n):
        if n == 0:
            tiles = [lambda k, t=t: row_of(0, k, 2 * gz + t) for t in range(2)]
            tiles.append(
                lambda k: jnp.where(
                    lane < 64,
                    row_of(0, k, lax.rem(2 * gz + 2, 8)),
                    row_of(0, k, lax.rem(2 * gz + 7, 8)),
                )
            )
        elif n == 1:
            tiles = [
                lambda k: row_of(1, k, gz),
                lambda k: jnp.where(
                    lane < 64,
                    row_of(1, k, lax.rem(gz + 1, 4)),
                    row_of(1, k, lax.rem(gz + 3, 4)),
                ),
            ]
        elif n == 2:

            def one(k):
                here, there = row_of(2, k, gz // 2), row_of(2, k, 1 - gz // 2)
                lower = jnp.where(lane < 96, here, there)
                upper = pltpu.roll(jnp.where(lane < 32, there, here), 64, 1)
                return jnp.where(lax.rem(gz, 2) == 0, lower, upper)

            tiles = [one]
        else:
            tiles = [lambda k: row_of(3, k, 0)]
        return [[tile(k) for k in range(5)] for tile in tiles]

    for n, level in enumerate(LEVELS):
        raw, ext, packed, received, halved = raws[n], exts[n], packs[n], receiveds[n], halveds[n]
        if n > 0:
            pack_faces(level, raw, packed)
            copies = {}
            order = sorted(offsets_of(level), key=lambda o: -sum(abs(i) for i in o))
            for offset in order:
                copies[offset] = remote(
                    *message(level, raw, packed, ext, received, offset), offset
                )
                copies[offset].start()
            pending += list(copies.values())
        coefs = level_coefs(n)
        for c in copies.values():
            c.wait_recv()
        begin(level, raw, received, ext, coefs)
        relax(level, ext, pings[n], pongs[n], coefs)
        if n == 0:
            stores = [
                pltpu.make_async_copy(
                    ping0.at[t, pl.ds(XO, 16), pl.ds(YO, 64), :],
                    smooth_ref.at[:, :, pl.ds(LANES * t, LANES)],
                    local.at[2 + t],
                )
                for t in range(2)
            ]
            for c in stores:
                c.start()
        residual_rows(level, ext, pings[n], coefs, pair, halved)
        if n == 0:
            total = select_dot(halved[0].reshape(256, LANES), halving(0, 0.5)) + select_dot(
                halved[1].reshape(256, LANES), halving(64, 0.5)
            )
            raw1[0] = total.reshape(8, 32, LANES)
        elif n == 1:
            raw2[0] = select_dot(halved[0].reshape(64, LANES), halving(0, 0.5)).reshape(
                4, 16, LANES
            )
        else:
            k = lax.broadcasted_iota(jnp.int32, (LANES, LANES), 0)
            picks = jnp.where(k < 64, halving(32 * gz, 0.5), 0.0)
            column[gz] = select_dot(halved[0].reshape(16, LANES), picks).reshape(2, 8, LANES)

    copies = [remote(column.at[gz], column.at[gz], offset) for offset in PROFILE_PEERS]
    for c in copies:
        c.start()
    pending += copies
    coefs = level_coefs(3)
    for c in copies:
        c.wait_recv()
    whole = (column[0] + column[1]) + (column[2] + column[3])
    slab[...] = whole
    strip = pl.ds(pl.multiple_of(8 + 8 * gy, 8), 8)
    copies = [
        remote(slab, ext3.at[0, pl.ds(8 - 2 * offset[0], 2), strip, :], offset)
        for offset in COLUMN_PEERS
    ]
    for c in copies:
        c.start()
    ext3[0, pl.ds(8, 2), strip, :] = whole
    for c in pending:
        c.wait_send()
    for c in copies:
        c.wait_recv()

    def wrapped(target, x, values):
        for j in range(6):
            target[0, x, pl.ds(8 * j, 8), :] = values[(j - 1) % 4]

    ext3[0, 16] = ext3[0, 0]

    def start_all(x, carry):
        wrapped(ext3, x, [ext3[0, x, pl.ds(8 + 8 * j, 8), :] * coefs[0][3] for j in range(4)])
        return carry

    lax.fori_loop(1, 17, start_all, 0)

    sweeps(1, ext3, ping3, pong3, 1, 17, COARSE_SWEEPS - 1, 4, coefs, wrapped)
    coarse_ref[...] = ping3[0, pl.ds(8, 2), pl.ds(8, 32), :]
    for c in copies:
        c.wait_send()
    for c in stores:
        c.wait()


def on_device(source, cell, face):
    f32 = jnp.float32
    messages = sum(len(offsets_of(level)) for level in LEVELS) + 6 + len(COLUMN_PEERS)
    vmem = pl.BlockSpec(memory_space=pltpu.VMEM)
    hbm = pl.BlockSpec(memory_space=pl.ANY)
    tile = (8, LANES)
    return pl.pallas_call(
        kernel,
        out_shape=(
            jax.ShapeDtypeStruct((16, 64, 256), f32),
            jax.ShapeDtypeStruct((2, 32, 128), f32),
        ),
        in_specs=[hbm, vmem, vmem],
        out_specs=(hbm, vmem),
        scratch_shapes=[
            pltpu.VMEM((2, 16, 64, LANES), f32),
            pltpu.VMEM((1, 8, 32, LANES), f32),
            pltpu.VMEM((1, 4, 16, LANES), f32),
            pltpu.VMEM(LEVELS[0]["shape"], f32),
            pltpu.VMEM(LEVELS[1]["shape"], f32),
            pltpu.VMEM(LEVELS[2]["shape"], f32),
            pltpu.VMEM((1, 18, 48, LANES), f32),
            pltpu.VMEM(LEVELS[0]["shape"], f32),
            pltpu.VMEM(LEVELS[1]["shape"], f32),
            pltpu.VMEM(LEVELS[2]["shape"], f32),
            pltpu.VMEM((1, 18, 48, LANES), f32),
            pltpu.VMEM(LEVELS[0]["shape"], f32),
            pltpu.VMEM(LEVELS[1]["shape"], f32),
            pltpu.VMEM(LEVELS[2]["shape"], f32),
            pltpu.VMEM((1, 18, 48, LANES), f32),
            pltpu.VMEM((2, 8) + tile, f32),
            pltpu.VMEM((1, 4) + tile, f32),
            pltpu.VMEM((1, 2) + tile, f32),
            pltpu.VMEM((2, 4, 10) + tile, f32),
            pltpu.VMEM((2, 3, 6) + tile, f32),
            pltpu.VMEM((2, 5, 4) + tile, f32),
            pltpu.VMEM((4,) + tile, f32),
            pltpu.VMEM((2,) + tile, f32),
            pltpu.VMEM((3, 16, LANES), f32),
            pltpu.VMEM((4, 5) + tile, f32),
            pltpu.VMEM((2, 64, LANES), f32),
            pltpu.VMEM((2, 8, 32, LANES), f32),
            pltpu.VMEM((1, 4, 16, LANES), f32),
            pltpu.VMEM((1, 2, 8, LANES), f32),
            pltpu.VMEM((4, 2) + tile, f32),
            pltpu.VMEM((2,) + tile, f32),
            pltpu.SemaphoreType.DMA((messages,)),
            pltpu.SemaphoreType.DMA((messages,)),
            pltpu.SemaphoreType.DMA((4,)),
            pltpu.SemaphoreType.REGULAR((2,)),
        ],
        compiler_params=pltpu.CompilerParams(
            collective_id=0, has_side_effects=True, vmem_limit_bytes=48 << 20
        ),
    )(source, cell, face)


def solution(mesh):
    return jax.shard_map(
        on_device,
        mesh=mesh,
        in_specs=(P("gx", "gy", "gz"), P("gz"), P("gz")),
        out_specs=(P("gx", "gy", "gz"), P("gx", None, None)),
        check_vma=False,
    )
```

```python
import jax
import jax.numpy as jnp
from jax import lax
from jax.experimental import pallas as pl
from jax.experimental.pallas import tpu as pltpu
from jax.sharding import PartitionSpec as P

MESH = pl.DeviceIdType.MESH
AXES = ("gx", "gy", "gz")
COUNTS = (8, 4, 4)
SWEEPS = 6
COARSE_SWEEPS = 8
HALO = 6
XO = 8
YO = 16
LANES = 128
DAMPING = 0.8

LEVELS = (
    dict(x=16, y=64, own=2, tiles=3, block=8, reach=1, step=1, shape=(3, 32, 96, LANES)),
    dict(x=8, y=32, own=1, tiles=2, block=8, reach=1, step=2, shape=(2, 24, 64, LANES)),
    dict(x=4, y=16, own=1, tiles=1, block=4, reach=2, step=0, shape=(1, 20, 48, LANES)),
)


def coordinates():
    return tuple(lax.axis_index(a) for a in AXES)


def device_at(place, offset):
    return tuple(
        lax.rem(p + (o + n), n) if o else p for p, o, n in zip(place, offset, COUNTS)
    )


def offsets_of(level):
    reach = level["reach"]
    return [
        (dx, dy, dz)
        for dx in range(-reach, reach + 1)
        for dy in (-1, 0, 1)
        for dz in (-1, 0, 1)
        if (dx, dy, dz) != (0, 0, 0)
    ]


FACES = ((1, 0, 0), (-1, 0, 0), (0, 1, 0), (0, -1, 0), (0, 0, 1), (0, 0, -1))
PROFILE_PEERS = ((0, 0, 1), (0, 0, -1), (0, 0, 2))
COLUMN_PEERS = tuple(
    (dx, dy, 0) for dx in (4, 3, -3, 2, -2, 1, -1, 0) for dy in (2, 1, -1, 0) if (dx, dy) != (0, 0)
)


def lane_iota(rows=8):
    return lax.broadcasted_iota(jnp.int32, (rows, LANES), 1)


def select_dot(rows, picks):
    return jnp.dot(
        rows, picks, preferred_element_type=jnp.float32, precision=lax.Precision.HIGHEST
    )


def halving(shift, value, parity=None):
    k = lax.broadcasted_iota(jnp.int32, (LANES, LANES), 0)
    l = 2 * (lax.broadcasted_iota(jnp.int32, (LANES, LANES), 1) - shift)
    if parity is None:
        hit = (k == l) | (k == l + 1)
    else:
        hit = k == l + parity
    return jnp.where(hit, jnp.float32(value), jnp.float32(0.0))


def message(level, raw, packed, ext, received, offset):
    dx, dy, dz = offset
    nx, ny, own = level["x"], level["y"], level["own"]
    if dz == 0:
        if dx == 0:
            sx, tx, width = 0, XO, nx
        elif dx > 0:
            width = min(nx, HALO - (dx - 1) * nx)
            sx, tx = nx - width, XO - (dx - 1) * nx - width
        else:
            width = min(nx, HALO - (-dx - 1) * nx)
            sx, tx = 0, XO + nx + (-dx - 1) * nx
        if dy == 0:
            sy, ty, rows = 0, YO, ny
        elif dy > 0:
            sy, ty, rows = ny - 8, YO - 8, 8
        else:
            sy, ty, rows = 0, YO + ny, 8
        return (
            raw.at[pl.ds(0, own), pl.ds(sx, width), pl.ds(sy, rows), :],
            ext.at[pl.ds(0, own), pl.ds(tx, width), pl.ds(ty, rows), :],
        )
    blocks, strips, reach = nx // level["block"], ny // 8, level["reach"]
    if dx == 0:
        sb, tb, nb = 0, reach, blocks
    elif dx > 0:
        sb, tb, nb = blocks - 1, reach - dx, 1
    else:
        sb, tb, nb = 0, reach + blocks - 1 - dx, 1
    if dy == 0:
        ss, ts, ns = 0, 1, strips
    elif dy > 0:
        ss, ts, ns = strips - 1, 0, 1
    else:
        ss, ts, ns = 0, strips + 1, 1
    return (
        packed.at[pl.ds(sb, nb), pl.ds(ss, ns), :, :],
        received.at[0 if dz > 0 else 1, pl.ds(tb, nb), pl.ds(ts, ns), :, :],
    )


def pack_faces(level, raw, packed):
    lane = lane_iota()
    group = lane // 8
    own, block, strips = level["own"], level["block"], level["y"] // 8
    far = 15 if level["tiles"] > 1 else 7

    def strip(s, carry):
        rows = pl.ds(pl.multiple_of(8 * s, 8), 8)
        for b in range(level["x"] // block):
            total = jnp.zeros((8, LANES), jnp.float32)
            for i in range(block):
                ends = raw[0, b * block + i, rows, :]
                if own == 2:
                    ends = jnp.where(lane < 64, ends, raw[1, b * block + i, rows, :])
                moved = pltpu.roll(ends, 16 * i, 1) if i else ends
                mine = (group == 2 * i) | (group == (2 * i + far) % 16)
                total = jnp.where(mine, moved, total)
            packed[b, s] = total
        return carry

    lax.fori_loop(0, strips, strip, 0)


def stencil(level_tiles, wanted, ext, x, row, coefs):
    lane = lane_iota()
    centre = [ext[t, x, pl.ds(row, 8), :] for t in range(level_tiles)]
    up = [pltpu.roll(v, 1, 1) for v in centre]
    down = [pltpu.roll(v, LANES - 1, 1) for v in centre]
    sums = []
    for t in range(wanted):
        beneath, overhead = up[t], down[t]
        if level_tiles > 1:
            beneath = jnp.where(lane == 0, up[t - 1], beneath)
            overhead = jnp.where(lane == LANES - 1, down[(t + 1) % level_tiles], overhead)
        around = (
            ext[t, x - 1, pl.ds(row, 8), :] + ext[t, x + 1, pl.ds(row, 8), :]
        ) + (ext[t, x, pl.ds(row - 1, 8), :] + ext[t, x, pl.ds(row + 1, 8), :])
        c, low, high, _, _ = coefs[t]
        sums.append(c * around + (low * beneath + high * overhead))
    return centre, sums


def update(tiles, beta, source, target, first, last, step, strips, coefs, finish):
    def planes(start):
        done = []
        for k in range(step):
            x = start + k
            values = []
            for j in range(strips):
                row = 8 + 8 * j
                centre, sums = stencil(tiles, tiles, source, x, row, coefs)
                for t in range(tiles):
                    if source is beta:
                        values.append(1.2 * centre[t] + sums[t])
                    else:
                        values.append((0.2 * centre[t] + beta[t, x, pl.ds(row, 8), :]) + sums[t])
            done.append((x, values))
        for x, values in done:
            finish(target, x, values)

    for_each(first, last, step, planes)


def for_each(first, last, step, body):
    if isinstance(first, int) and last - first == step:
        body(first)
        return

    def turn(i, carry):
        body(first + step * i)
        return carry

    lax.fori_loop(0, (last - first) // step, turn, 0)


def sweeps(tiles, beta, ping, pong, first, last, count, step, strips, coefs, finish):
    if step == 0:
        source = beta
        for s in range(1, count + 1):
            target = ping if s % 2 else pong
            lo, hi = first + s, last - s
            update(tiles, beta, source, target, lo, hi, hi - lo, strips, coefs, finish)
            source = target
        return
    update(tiles, beta, beta, ping, first + 1, last - 1, step, strips, coefs, finish)

    def two(k, carry):
        s = 2 * k + 2
        update(tiles, beta, ping, pong, first + s, last - s, step, strips, coefs, finish)
        update(tiles, beta, pong, ping, first + s + 1, last - s - 1, step, strips, coefs, finish)
        return carry

    lax.fori_loop(0, (count - 1) // 2, two, 0)


def relax(level, ext, ping, pong, coefs):
    tiles, nx, strips = level["tiles"], level["x"], level["y"] // 8 + 2

    def finish(target, x, values):
        for j in range(strips):
            for t in range(tiles):
                target[t, x, pl.ds(8 + 8 * j, 8), :] = values[j * tiles + t]

    sweeps(
        tiles,
        ext,
        ping,
        pong,
        XO - HALO,
        XO + nx + HALO,
        SWEEPS - 1,
        level["step"],
        strips,
        coefs,
        finish,
    )


def begin(level, raw, received, ext, coefs):
    tiles, own, nx, block = level["tiles"], level["own"], level["x"], level["block"]
    strips, step = level["y"] // 8 + 2, max(level["step"], 2)
    lane = lane_iota()
    even = lax.rem(lane // 8, 2) == 0
    base = 64 if tiles == 1 else 0

    def halo_tile(x, j):
        e, i = x // block, lax.rem(x, block)
        both = jnp.where(even, received[1, e, j], received[0, e, j])
        return pltpu.roll(both, lax.rem(base + LANES - 16 * i, LANES), 1)

    def plane_of(inside):
        def plane(x):
            for j in range(strips):
                row = 8 + 8 * j
                ends = halo_tile(x, j)
                for t in range(own):
                    if inside and 0 < j < strips - 1:
                        b = raw[t, x - XO, pl.ds(8 * (j - 1), 8), :]
                    else:
                        b = ext[t, x, pl.ds(row, 8), :]
                    if tiles == 1:
                        b = jnp.where(lane < 64, b, ends)
                    ext[t, x, pl.ds(row, 8), :] = b * coefs[t][3]
                if tiles > 1:
                    ext[own, x, pl.ds(row, 8), :] = ends * coefs[own][3]

        def some(x):
            for k in range(step):
                plane(x + k)

        return some

    for_each(XO - HALO, XO, step, plane_of(False))
    for_each(XO, XO + nx, step, plane_of(True))
    for_each(XO + nx, XO + nx + HALO, step, plane_of(False))


def residual_rows(level, ext, ping, coefs, pair, halved):
    tiles, own, nx, ny = level["tiles"], level["own"], level["x"], level["y"]

    def planes(p, carry):
        for j in range(ny // 8):
            row = YO + 8 * j
            total = [None] * own
            for k in range(2):
                x = XO + 2 * p + k
                centre, sums = stencil(tiles, own, ping, x, row, coefs)
                for t in range(own):
                    beta = ext[t, x, pl.ds(row, 8), :]
                    r = (beta - 0.8 * centre[t]) + sums[t]
                    total[t] = r if k == 0 else total[t] + r
            for t in range(own):
                pair[t, pl.ds(8 * j, 8), :] = total[t] * coefs[t][4]
        for t in range(own):
            halved[t, p] = (
                pair[t, pl.ds(0, ny // 2, stride=2), :] + pair[t, pl.ds(1, ny // 2, stride=2), :]
            )
        return carry

    lax.fori_loop(0, nx // 2, planes, 0)


def kernel(
    source_ref,
    cell_ref,
    face_ref,
    smooth_ref,
    coarse_ref,
    raw0,
    raw1,
    raw2,
    ext0,
    ext1,
    ext2,
    ext3,
    ping0,
    ping1,
    ping2,
    ping3,
    pong0,
    pong1,
    pong2,
    pong3,
    packed0,
    packed1,
    packed2,
    received0,
    received1,
    received2,
    line,
    profile,
    tables,
    spread,
    constants,
    pair,
    halved0,
    halved1,
    halved2,
    column,
    slab,
    send,
    recv,
    local,
    greet,
):
    place = coordinates()
    gx, gy, gz = place
    counter = [0]

    def remote(source, target, offset):
        k = counter[0]
        counter[0] += 1
        return pltpu.make_async_remote_copy(
            src_ref=source,
            dst_ref=target,
            send_sem=send.at[k],
            recv_sem=recv.at[k],
            device_id=device_at(place, offset),
            device_id_type=MESH,
        )

    pings, pongs = (ping0, ping1, ping2), (pong0, pong1, pong2)
    raws, exts = (raw0, raw1, raw2), (ext0, ext1, ext2)
    packs, receiveds = (packed0, packed1, packed2), (received0, received1, received2)
    halveds = (halved0, halved1, halved2)

    barrier = pltpu.get_barrier_semaphore()
    peers = FACES + ((0, 0, 2),)
    for offset in peers:
        pl.semaphore_signal(
            barrier, inc=1, device_id=device_at(place, offset), device_id_type=MESH
        )
    loads = [
        pltpu.make_async_copy(
            source_ref.at[:, :, pl.ds(LANES * t, LANES)], raw0.at[t], local.at[t]
        )
        for t in range(2)
    ]
    loads.append(pltpu.make_async_copy(cell_ref, line.at[0], local.at[4]))
    loads.append(pltpu.make_async_copy(face_ref, line.at[1], local.at[5]))
    for c in loads:
        c.start()
    mine = profile.at[gz]
    for c in loads:
        c.wait()
    for t in range(2):
        profile[gz, pl.ds(t, 1), :] = line[0, pl.ds(LANES * t, LANES)].reshape(1, LANES)
        profile[gz, pl.ds(2 + t, 1), :] = line[1, pl.ds(LANES * t, LANES)].reshape(1, LANES)
    pack_faces(LEVELS[0], raw0, packed0)
    pl.semaphore_wait(barrier, len(peers))

    pending = []
    copies = {}
    for offset in offsets_of(LEVELS[0]):
        copies[offset] = remote(
            *message(LEVELS[0], raw0, packed0, ext0, received0, offset), offset
        )
    profiles = [remote(mine, mine, offset) for offset in PROFILE_PEERS]
    for offset in FACES:
        copies[offset].start()
    for c in profiles:
        c.start()
    for stage, distance in ((0, 2), (1, 3)):
        for offset in FACES:
            pl.semaphore_signal(
                greet.at[stage], inc=1, device_id=device_at(place, offset), device_id_type=MESH
            )
        pl.semaphore_wait(greet.at[stage], len(FACES))
        for offset in copies:
            if sum(abs(o) for o in offset) == distance:
                copies[offset].start()
    pending += list(copies.values()) + profiles

    for c in profiles:
        c.wait_recv()
    lane = lane_iota()
    row = lax.broadcasted_iota(jnp.int32, (8, LANES), 0)
    for z in range(4):
        for t in range(2):
            tables[0, pl.ds(2 * z + t, 1), :] = profile[z, pl.ds(t, 1), :]
            tables[1, pl.ds(2 * z + t, 1), :] = profile[z, pl.ds(2 + t, 1), :]
    cell, below = tables[0], tables[1]
    turned = pltpu.roll(below, LANES - 1, 1)
    above = jnp.where(lane == LANES - 1, pltpu.roll(turned, 7, 0), turned)
    above = jnp.where((row == 7) & (lane == LANES - 1), 0.0, above)
    first, second = halving(0, 1.0, 0), halving(0, 1.0, 1)
    first, second = first + halving(64, 1.0, 0), second + halving(64, 1.0, 1)
    for n in range(4):
        scale = DAMPING / (4.0 * cell + below + above)
        constants[n, 0] = cell * scale
        constants[n, 1] = jnp.where((row == 0) & (lane == 0), 0.0, below * scale)
        constants[n, 2] = above * scale
        constants[n, 3] = scale
        constants[n, 4] = (4.0 * cell + below + above) * (1.0 / DAMPING)
        if n < 3:
            spread[0, pl.ds(0, 8), :] = 0.5 * (select_dot(cell, first) + select_dot(cell, second))
            spread[1, pl.ds(0, 8), :] = select_dot(below, first)
            spread[2, pl.ds(0, 8), :] = select_dot(above, second)
            narrow = [
                jnp.where(
                    lane < 64,
                    spread[k, pl.ds(0, 8, stride=2), :],
                    spread[k, pl.ds(1, 8, stride=2), :],
                )
                for k in range(3)
            ]
            used = row < 8 >> (n + 1)
            cell, below = jnp.where(used, narrow[0], 1.0), jnp.where(used, narrow[1], 1.0)
            above = jnp.where(used, narrow[2], 1.0)

    def row_of(n, k, r):
        return jnp.broadcast_to(constants[n, k, pl.ds(r, 1), :], (8, LANES))

    def level_coefs(n):
        if n == 0:
            tiles = [lambda k, t=t: row_of(0, k, 2 * gz + t) for t in range(2)]
            tiles.append(
                lambda k: jnp.where(
                    lane < 64,
                    row_of(0, k, lax.rem(2 * gz + 2, 8)),
                    row_of(0, k, lax.rem(2 * gz + 7, 8)),
                )
            )
        elif n == 1:
            tiles = [
                lambda k: row_of(1, k, gz),
                lambda k: jnp.where(
                    lane < 64,
                    row_of(1, k, lax.rem(gz + 1, 4)),
                    row_of(1, k, lax.rem(gz + 3, 4)),
                ),
            ]
        elif n == 2:

            def one(k):
                here, there = row_of(2, k, gz // 2), row_of(2, k, 1 - gz // 2)
                lower = jnp.where(lane < 96, here, there)
                upper = pltpu.roll(jnp.where(lane < 32, there, here), 64, 1)
                return jnp.where(lax.rem(gz, 2) == 0, lower, upper)

            tiles = [one]
        else:
            tiles = [lambda k: row_of(3, k, 0)]
        return [[tile(k) for k in range(5)] for tile in tiles]

    for n, level in enumerate(LEVELS):
        raw, ext, packed, received, halved = raws[n], exts[n], packs[n], receiveds[n], halveds[n]
        if n > 0:
            pack_faces(level, raw, packed)
            copies = {}
            order = sorted(offsets_of(level), key=lambda o: -sum(abs(i) for i in o))
            for offset in order:
                copies[offset] = remote(
                    *message(level, raw, packed, ext, received, offset), offset
                )
                copies[offset].start()
            pending += list(copies.values())
        coefs = level_coefs(n)
        for c in copies.values():
            c.wait_recv()
        begin(level, raw, received, ext, coefs)
        relax(level, ext, pings[n], pongs[n], coefs)
        if n == 0:
            stores = [
                pltpu.make_async_copy(
                    ping0.at[t, pl.ds(XO, 16), pl.ds(YO, 64), :],
                    smooth_ref.at[:, :, pl.ds(LANES * t, LANES)],
                    local.at[2 + t],
                )
                for t in range(2)
            ]
            for c in stores:
                c.start()
        residual_rows(level, ext, pings[n], coefs, pair, halved)
        if n == 0:
            total = select_dot(halved[0].reshape(256, LANES), halving(0, 0.5)) + select_dot(
                halved[1].reshape(256, LANES), halving(64, 0.5)
            )
            raw1[0] = total.reshape(8, 32, LANES)
        elif n == 1:
            raw2[0] = select_dot(halved[0].reshape(64, LANES), halving(0, 0.5)).reshape(
                4, 16, LANES
            )
        else:
            k = lax.broadcasted_iota(jnp.int32, (LANES, LANES), 0)
            picks = jnp.where(k < 64, halving(32 * gz, 0.5), 0.0)
            column[gz] = select_dot(halved[0].reshape(16, LANES), picks).reshape(2, 8, LANES)

    copies = [remote(column.at[gz], column.at[gz], offset) for offset in PROFILE_PEERS]
    for c in copies:
        c.start()
    pending += copies
    coefs = level_coefs(3)
    for c in copies:
        c.wait_recv()
    whole = (column[0] + column[1]) + (column[2] + column[3])
    slab[...] = whole
    strip = pl.ds(pl.multiple_of(8 + 8 * gy, 8), 8)
    copies = [
        remote(slab, ext3.at[0, pl.ds(8 - 2 * offset[0], 2), strip, :], offset)
        for offset in COLUMN_PEERS
    ]
    for c in copies:
        c.start()
    ext3[0, pl.ds(8, 2), strip, :] = whole
    for c in pending:
        c.wait_send()
    for c in copies:
        c.wait_recv()

    def wrapped(target, x, values):
        for j in range(6):
            target[0, x, pl.ds(8 * j, 8), :] = values[(j - 1) % 4]

    ext3[0, 16] = ext3[0, 0]

    def start_all(x, carry):
        wrapped(ext3, x, [ext3[0, x, pl.ds(8 + 8 * j, 8), :] * coefs[0][3] for j in range(4)])
        return carry

    lax.fori_loop(1, 17, start_all, 0)

    sweeps(1, ext3, ping3, pong3, 1, 17, COARSE_SWEEPS - 1, 0, 4, coefs, wrapped)
    coarse_ref[...] = ping3[0, pl.ds(8, 2), pl.ds(8, 32), :]
    for c in copies:
        c.wait_send()
    for c in stores:
        c.wait()


def on_device(source, cell, face):
    f32 = jnp.float32
    messages = sum(len(offsets_of(level)) for level in LEVELS) + 6 + len(COLUMN_PEERS)
    vmem = pl.BlockSpec(memory_space=pltpu.VMEM)
    hbm = pl.BlockSpec(memory_space=pltpu.HBM)
    tile = (8, LANES)
    return pl.pallas_call(
        kernel,
        out_shape=(
            jax.ShapeDtypeStruct((16, 64, 256), f32),
            jax.ShapeDtypeStruct((2, 32, 128), f32),
        ),
        in_specs=[hbm, hbm, hbm],
        out_specs=(hbm, vmem),
        scratch_shapes=[
            pltpu.VMEM((2, 16, 64, LANES), f32),
            pltpu.VMEM((1, 8, 32, LANES), f32),
            pltpu.VMEM((1, 4, 16, LANES), f32),
            pltpu.VMEM(LEVELS[0]["shape"], f32),
            pltpu.VMEM(LEVELS[1]["shape"], f32),
            pltpu.VMEM(LEVELS[2]["shape"], f32),
            pltpu.VMEM((1, 18, 48, LANES), f32),
            pltpu.VMEM(LEVELS[0]["shape"], f32),
            pltpu.VMEM(LEVELS[1]["shape"], f32),
            pltpu.VMEM(LEVELS[2]["shape"], f32),
            pltpu.VMEM((1, 18, 48, LANES), f32),
            pltpu.VMEM(LEVELS[0]["shape"], f32),
            pltpu.VMEM(LEVELS[1]["shape"], f32),
            pltpu.VMEM(LEVELS[2]["shape"], f32),
            pltpu.VMEM((1, 18, 48, LANES), f32),
            pltpu.VMEM((2, 8) + tile, f32),
            pltpu.VMEM((1, 4) + tile, f32),
            pltpu.VMEM((1, 2) + tile, f32),
            pltpu.VMEM((2, 4, 10) + tile, f32),
            pltpu.VMEM((2, 3, 6) + tile, f32),
            pltpu.VMEM((2, 5, 4) + tile, f32),
            pltpu.VMEM((2, 256), f32),
            pltpu.VMEM((4,) + tile, f32),
            pltpu.VMEM((2,) + tile, f32),
            pltpu.VMEM((3, 16, LANES), f32),
            pltpu.VMEM((4, 5) + tile, f32),
            pltpu.VMEM((2, 64, LANES), f32),
            pltpu.VMEM((2, 8, 32, LANES), f32),
            pltpu.VMEM((1, 4, 16, LANES), f32),
            pltpu.VMEM((1, 2, 8, LANES), f32),
            pltpu.VMEM((4, 2) + tile, f32),
            pltpu.VMEM((2,) + tile, f32),
            pltpu.SemaphoreType.DMA((messages,)),
            pltpu.SemaphoreType.DMA((messages,)),
            pltpu.SemaphoreType.DMA((6,)),
            pltpu.SemaphoreType.REGULAR((2,)),
        ],
        compiler_params=pltpu.CompilerParams(
            collective_id=0, has_side_effects=True, vmem_limit_bytes=62 << 20
        ),
    )(source, cell, face)


def solution(mesh):
    return jax.shard_map(
        on_device,
        mesh=mesh,
        in_specs=(P("gx", "gy", "gz"), P("gz"), P("gz")),
        out_specs=(P("gx", "gy", "gz"), P("gx", None, None)),
        check_vma=False,
    )
```

```python
import jax
import jax.numpy as jnp
from jax import lax
from jax.experimental import pallas as pl
from jax.experimental.pallas import tpu as pltpu
from jax.sharding import PartitionSpec as P

MESH = pl.DeviceIdType.MESH
AXES = ("gx", "gy", "gz")
COUNTS = (8, 4, 4)
SWEEPS = 6
COARSE_SWEEPS = 8
HALO = 6
XO = 8
YO = 16
LANES = 128
DAMPING = 0.8

LEVELS = (
    dict(x=16, y=64, own=2, split=True, tiles=3, block=8, reach=1, step=1, shape=(3, 32, 96, LANES)),
    dict(x=8, y=32, own=1, split=False, tiles=2, block=8, reach=1, step=2, shape=(2, 24, 64, LANES)),
    dict(x=4, y=16, own=1, split=False, tiles=1, block=4, reach=2, step=0, shape=(1, 20, 48, LANES)),
)


def coordinates():
    return tuple(lax.axis_index(a) for a in AXES)


def device_at(place, offset):
    return tuple(
        lax.rem(p + (o + n), n) if o else p for p, o, n in zip(place, offset, COUNTS)
    )


def offsets_of(level):
    reach = level["reach"]
    return [
        (dx, dy, dz)
        for dx in range(-reach, reach + 1)
        for dy in (-1, 0, 1)
        for dz in (-1, 0, 1)
        if (dx, dy, dz) != (0, 0, 0)
    ]


FACES = ((1, 0, 0), (-1, 0, 0), (0, 1, 0), (0, -1, 0), (0, 0, 1), (0, 0, -1))
PROFILE_PEERS = ((0, 0, 1), (0, 0, -1), (0, 0, 2))
COLUMN_PEERS = tuple(
    (dx, dy, 0) for dx in (4, 3, -3, 2, -2, 1, -1, 0) for dy in (2, 1, -1, 0) if (dx, dy) != (0, 0)
)


def lane_iota(rows=8):
    return lax.broadcasted_iota(jnp.int32, (rows, LANES), 1)


def select_dot(rows, picks):
    return jnp.dot(
        rows, picks, preferred_element_type=jnp.float32, precision=lax.Precision.HIGHEST
    )


def as_bf16(hit):
    return jnp.where(hit, jnp.float32(1.0), jnp.float32(0.0)).astype(jnp.bfloat16)


def permuted(first, second, picks):
    rows = first.size // LANES
    left = jnp.concatenate([first.reshape(rows, LANES), second.reshape(rows, LANES)], axis=1)
    total = None
    for _ in range(3):
        term = left.astype(jnp.bfloat16)
        left = left - term.astype(jnp.float32)
        part = jnp.dot(term, picks, preferred_element_type=jnp.float32)
        total = part if total is None else total + part
    return total


def halving(shift, value, parity=None):
    k = lax.broadcasted_iota(jnp.int32, (LANES, LANES), 0)
    l = 2 * (lax.broadcasted_iota(jnp.int32, (LANES, LANES), 1) - shift)
    if parity is None:
        hit = (k == l) | (k == l + 1)
    else:
        hit = k == l + parity
    return jnp.where(hit, jnp.float32(value), jnp.float32(0.0))


def message(level, raw, packed, ext, received, offset):
    dx, dy, dz = offset
    nx, ny, own = level["x"], level["y"], level["own"]
    if dz == 0:
        if dx == 0:
            sx, tx, width = 0, XO, nx
        elif dx > 0:
            width = min(nx, HALO - (dx - 1) * nx)
            sx, tx = nx - width, XO - (dx - 1) * nx - width
        else:
            width = min(nx, HALO - (-dx - 1) * nx)
            sx, tx = 0, XO + nx + (-dx - 1) * nx
        if dy == 0:
            sy, ty, rows = 0, YO, ny
        elif dy > 0:
            sy, ty, rows = ny - 8, YO - 8, 8
        else:
            sy, ty, rows = 0, YO + ny, 8
        return (
            raw.at[pl.ds(0, own), pl.ds(sx, width), pl.ds(sy, rows), :],
            ext.at[pl.ds(0, own), pl.ds(tx, width), pl.ds(ty, rows), :],
        )
    blocks, strips, reach = nx // level["block"], ny // 8, level["reach"]
    if dx == 0:
        sb, tb, nb = 0, reach, blocks
    elif dx > 0:
        sb, tb, nb = blocks - 1, reach - dx, 1
    else:
        sb, tb, nb = 0, reach + blocks - 1 - dx, 1
    if dy == 0:
        ss, ts, ns = 0, 1, strips
    elif dy > 0:
        ss, ts, ns = strips - 1, 0, 1
    else:
        ss, ts, ns = 0, strips + 1, 1
    return (
        packed.at[pl.ds(sb, nb), pl.ds(ss, ns), :, :],
        received.at[0 if dz > 0 else 1, pl.ds(tb, nb), pl.ds(ts, ns), :, :],
    )


def pack_faces(level, raw, packed):
    lane = lane_iota()
    group = lane // 8
    own, block, strips = level["own"], level["block"], level["y"] // 8
    far = 15 if level["tiles"] > 1 else 7

    def strip(s, carry):
        rows = pl.ds(pl.multiple_of(8 * s, 8), 8)
        for b in range(level["x"] // block):
            total = jnp.zeros((8, LANES), jnp.float32)
            for i in range(block):
                ends = raw[0, b * block + i, rows, :]
                if own == 2:
                    ends = jnp.where(lane < 64, ends, raw[1, b * block + i, rows, :])
                moved = pltpu.roll(ends, 16 * i, 1) if i else ends
                mine = (group == 2 * i) | (group == (2 * i + far) % 16)
                total = jnp.where(mine, moved, total)
            packed[b, s] = total
        return carry

    lax.fori_loop(0, strips, strip, 0)


def vertical(level_tiles, wanted, centre):
    lane = lane_iota()

    def up(v):
        return pltpu.roll(v, 1, 1)

    def down(v):
        return pltpu.roll(v, LANES - 1, 1)

    if level_tiles == 1:
        return [(up(centre[0]), down(centre[0]))]
    if level_tiles == 2:
        ups, downs = [up(v) for v in centre], [down(v) for v in centre]
        return [
            (
                jnp.where(lane == 0, ups[1 - t], ups[t]),
                jnp.where(lane == LANES - 1, downs[1 - t], downs[t]),
            )
            for t in range(wanted)
        ]
    even, odd, halo = centre
    up_odd, down_even, up_halo, down_halo = up(odd), down(even), up(halo), down(halo)
    return [
        (jnp.where(lane == 0, up_halo, up_odd), odd),
        (even, jnp.where(lane == LANES - 1, down_halo, down_even)),
        (
            jnp.where(lane == 0, up_odd, up_halo),
            jnp.where(lane == LANES - 1, down_even, down_halo),
        ),
    ][:wanted]


def stencil(level_tiles, wanted, ext, x, row, coefs):
    centre = [ext[t, x, pl.ds(row, 8), :] for t in range(level_tiles)]
    sums = []
    for t, (beneath, overhead) in enumerate(vertical(level_tiles, wanted, centre)):
        around = (
            ext[t, x - 1, pl.ds(row, 8), :] + ext[t, x + 1, pl.ds(row, 8), :]
        ) + (ext[t, x, pl.ds(row - 1, 8), :] + ext[t, x, pl.ds(row + 1, 8), :])
        c, low, high, _, _ = coefs[t]
        sums.append(c * around + (low * beneath + high * overhead))
    return centre, sums


def update(tiles, beta, source, target, first, last, step, strips, coefs, finish):
    def planes(start):
        done = []
        for k in range(step):
            x = start + k
            values = []
            for j in range(strips):
                row = 8 + 8 * j
                centre, sums = stencil(tiles, tiles, source, x, row, coefs)
                for t in range(tiles):
                    if source is beta:
                        values.append(1.2 * centre[t] + sums[t])
                    else:
                        values.append((0.2 * centre[t] + beta[t, x, pl.ds(row, 8), :]) + sums[t])
            done.append((x, values))
        for x, values in done:
            finish(target, x, values)

    for_each(first, last, step, planes)


def for_each(first, last, step, body):
    if isinstance(first, int) and last - first == step:
        body(first)
        return

    def turn(i, carry):
        body(first + step * i)
        return carry

    lax.fori_loop(0, (last - first) // step, turn, 0)


def sweeps(tiles, beta, ping, pong, first, last, count, step, strips, coefs, finish):
    if step == 0:
        source = beta
        for s in range(1, count + 1):
            target = ping if s % 2 else pong
            lo, hi = first + s, last - s
            update(tiles, beta, source, target, lo, hi, hi - lo, strips, coefs, finish)
            source = target
        return
    update(tiles, beta, beta, ping, first + 1, last - 1, step, strips, coefs, finish)

    def two(k, carry):
        s = 2 * k + 2
        update(tiles, beta, ping, pong, first + s, last - s, step, strips, coefs, finish)
        update(tiles, beta, pong, ping, first + s + 1, last - s - 1, step, strips, coefs, finish)
        return carry

    lax.fori_loop(0, (count - 1) // 2, two, 0)


def finisher(level):
    tiles, strips = level["tiles"], level["y"] // 8 + 2

    def finish(target, x, values):
        for j in range(strips):
            for t in range(tiles):
                target[t, x, pl.ds(8 + 8 * j, 8), :] = values[j * tiles + t]

    return finish


def relax(level, ext, ping, pong, coefs, reach):
    sweeps(
        level["tiles"],
        ext,
        ping,
        pong,
        XO - reach,
        XO + level["x"] + reach,
        SWEEPS - 1,
        level["step"],
        level["y"] // 8 + 2,
        coefs,
        finisher(level),
    )


def relax_wings(level, ext, ping, pong, coefs):
    tiles, nx, strips = level["tiles"], level["x"], level["y"] // 8 + 2
    finish = finisher(level)

    def both(s, source, target):
        for first in (XO - HALO + s, XO + nx - s):
            update(tiles, ext, source, target, first, first + HALO, 1, strips, coefs, finish)

    both(1, ext, ping)

    def two(k, carry):
        both(2 * k + 2, ping, pong)
        both(2 * k + 3, pong, ping)
        return carry

    lax.fori_loop(0, (SWEEPS - 2) // 2, two, 0)


def begin(level, raw, received, ext, coefs, parts):
    tiles, own, nx, block = level["tiles"], level["own"], level["x"], level["block"]
    strips, step = level["y"] // 8 + 2, max(level["step"], 2)
    lane = lane_iota()
    even = lax.rem(lane // 8, 2) == 0
    base = 64 if tiles == 1 else 0

    def halo_tile(x, j):
        e, i = x // block, lax.rem(x, block)
        both = jnp.where(even, received[1, e, j], received[0, e, j])
        return pltpu.roll(both, lax.rem(base + LANES - 16 * i, LANES), 1)

    def plane_of(inside):
        def plane(x):
            for j in range(strips):
                row = 8 + 8 * j
                ends = halo_tile(x, j)
                for t in range(own):
                    if inside and 0 < j < strips - 1:
                        b = raw[t, x - XO, pl.ds(8 * (j - 1), 8), :]
                    else:
                        b = ext[t, x, pl.ds(row, 8), :]
                    if tiles == 1:
                        b = jnp.where(lane < 64, b, ends)
                    ext[t, x, pl.ds(row, 8), :] = b * coefs[t][3]
                if tiles > 1:
                    ext[own, x, pl.ds(row, 8), :] = ends * coefs[own][3]

        def some(x):
            for k in range(step):
                plane(x + k)

        return some

    if "own" in parts:
        for_each(XO, XO + nx, step, plane_of(True))
    if "halo" in parts:
        for_each(XO - HALO, XO, step, plane_of(False))
        for_each(XO + nx, XO + nx + HALO, step, plane_of(False))


def residual_rows(level, ext, ping, coefs, pair, halved):
    tiles, own, nx, ny = level["tiles"], level["own"], level["x"], level["y"]

    def planes(p, carry):
        for j in range(ny // 8):
            row = YO + 8 * j
            total = [None] * own
            for k in range(2):
                x = XO + 2 * p + k
                centre, sums = stencil(tiles, own, ping, x, row, coefs)
                for t in range(own):
                    beta = ext[t, x, pl.ds(row, 8), :]
                    r = (beta - 0.8 * centre[t]) + sums[t]
                    total[t] = r if k == 0 else total[t] + r
            row_sum = total[0] * coefs[0][4]
            if own == 2:
                row_sum = row_sum + total[1] * coefs[1][4]
            pair[pl.ds(8 * j, 8), :] = row_sum
        halved[0, p] = 0.5 * (
            pair[pl.ds(0, ny // 2, stride=2), :] + pair[pl.ds(1, ny // 2, stride=2), :]
        )
        return carry

    lax.fori_loop(0, nx // 2, planes, 0)


def kernel(
    source_ref,
    cell_ref,
    face_ref,
    smooth_ref,
    coarse_ref,
    raw0,
    raw1,
    raw2,
    ext0,
    ext1,
    ext2,
    ext3,
    natural,
    sm,
    order,
    back,
    ping0,
    ping1,
    ping2,
    ping3,
    pong0,
    pong1,
    pong2,
    pong3,
    packed0,
    packed1,
    packed2,
    received0,
    received1,
    received2,
    line,
    profile,
    tables,
    spread,
    constants,
    sides,
    pair,
    halved1,
    halved2,
    column,
    slab,
    send,
    recv,
    local,
    greet,
):
    place = coordinates()
    gx, gy, gz = place
    counter = [0]

    def remote(source, target, offset):
        k = counter[0]
        counter[0] += 1
        return pltpu.make_async_remote_copy(
            src_ref=source,
            dst_ref=target,
            send_sem=send.at[k],
            recv_sem=recv.at[k],
            device_id=device_at(place, offset),
            device_id_type=MESH,
        )

    pings, pongs = (ping0, ping1, ping2), (pong0, pong1, pong2)
    raws, exts = (raw0, raw1, raw2), (ext0, ext1, ext2)
    packs, receiveds = (packed0, packed1, packed2), (received0, received1, received2)
    halveds = (raw1, halved1, halved2)

    barrier = pltpu.get_barrier_semaphore()
    peers = FACES + ((0, 0, 2),)
    for offset in peers:
        pl.semaphore_signal(
            barrier, inc=1, device_id=device_at(place, offset), device_id_type=MESH
        )
    loads = [
        pltpu.make_async_copy(
            source_ref.at[:, :, pl.ds(LANES * t, LANES)], natural.at[t], local.at[t]
        )
        for t in range(2)
    ]
    loads.append(pltpu.make_async_copy(cell_ref, line.at[0], local.at[4]))
    loads.append(pltpu.make_async_copy(face_ref, line.at[1], local.at[5]))
    for c in loads:
        c.start()
    mine = profile.at[gz]
    for c in loads:
        c.wait()
    for t in range(2):
        profile[gz, pl.ds(t, 1), :] = line[0, pl.ds(LANES * t, LANES)].reshape(1, LANES)
        profile[gz, pl.ds(2 + t, 1), :] = line[1, pl.ds(LANES * t, LANES)].reshape(1, LANES)
    z_from = lax.broadcasted_iota(jnp.int32, (256, 256), 0)
    z_to = lax.broadcasted_iota(jnp.int32, (256, 256), 1)
    order[...] = as_bf16(z_from == 2 * lax.rem(z_to, LANES) + z_to // LANES)
    back[...] = as_bf16(z_to == 2 * lax.rem(z_from, LANES) + z_from // LANES)

    def sort_cells(g, carry):
        at = pl.ds(4 * g, 4)
        moved = permuted(natural[0, at], natural[1, at], order[...])
        raw0[0, at] = moved[:, :LANES].reshape(4, 64, LANES)
        raw0[1, at] = moved[:, LANES:].reshape(4, 64, LANES)
        return carry

    lax.fori_loop(0, 4, sort_cells, 0)
    pack_faces(LEVELS[0], natural, packed0)
    pl.semaphore_wait(barrier, len(peers))

    pending = []
    copies = {}
    for offset in offsets_of(LEVELS[0]):
        copies[offset] = remote(
            *message(LEVELS[0], raw0, packed0, ext0, received0, offset), offset
        )
    profiles = [remote(mine, mine, offset) for offset in PROFILE_PEERS]
    for c in profiles:
        c.start()
    for offset in FACES[:1:-1]:
        copies[offset].start()
    for stage, distance in ((0, 2), (1, 3)):
        for offset in FACES:
            pl.semaphore_signal(
                greet.at[stage], inc=1, device_id=device_at(place, offset), device_id_type=MESH
            )
        pl.semaphore_wait(greet.at[stage], len(FACES))
        for offset in sorted(copies, key=lambda o: abs(o[0])):
            if sum(abs(o) for o in offset) == distance:
                copies[offset].start()
            elif distance == 2 and offset in FACES[:2]:
                copies[offset].start()
    pending += list(copies.values()) + profiles

    for c in profiles:
        c.wait_recv()
    lane = lane_iota()
    row = lax.broadcasted_iota(jnp.int32, (8, LANES), 0)
    for z in range(4):
        for t in range(2):
            tables[0, pl.ds(2 * z + t, 1), :] = profile[z, pl.ds(t, 1), :]
            tables[1, pl.ds(2 * z + t, 1), :] = profile[z, pl.ds(2 + t, 1), :]
    cell, below = tables[0], tables[1]
    turned = pltpu.roll(below, LANES - 1, 1)
    above = jnp.where(lane == LANES - 1, pltpu.roll(turned, 7, 0), turned)
    above = jnp.where((row == 7) & (lane == LANES - 1), 0.0, above)
    first, second = halving(0, 1.0, 0), halving(0, 1.0, 1)
    first, second = first + halving(64, 1.0, 0), second + halving(64, 1.0, 1)
    picks = jnp.concatenate([first, second], axis=1)

    def keep(ref, cell, below, above, bottom):
        diag = 4.0 * cell + below + above
        scale = DAMPING / diag
        ref[0] = cell * scale
        ref[1] = jnp.where((row == 0) & (lane == 0), 0.0, below * scale) if bottom else below * scale
        ref[2] = above * scale
        ref[3] = scale
        ref[4] = diag * (1.0 / DAMPING)

    def narrowed(n, fields):
        halves = []
        for k, values in enumerate(fields):
            taken = select_dot(values, picks)
            for p in range(2):
                spread[k, p, pl.ds(0, 8), :] = taken[:, LANES * p : LANES * (p + 1)]
        for k in range(3):
            halves.append(
                [
                    jnp.where(
                        row < 8 >> (n + 1),
                        jnp.where(
                            lane < 64,
                            spread[k, p, pl.ds(0, 8, stride=2), :],
                            spread[k, p, pl.ds(1, 8, stride=2), :],
                        ),
                        1.0,
                    )
                    for p in range(2)
                ]
            )
        return halves

    keep(constants.at[0], cell, below, above, True)
    finest = narrowed(0, (cell, below, above))
    for p in range(2):
        keep(sides.at[p], *[field[p] for field in finest], p == 0)

    def coarser_constants():
        halves = finest
        for n in range(1, 4):
            cells, belows, aboves = halves
            fields = (0.5 * (cells[0] + cells[1]), belows[0], aboves[1])
            keep(constants.at[n], *fields, True)
            if n < 3:
                halves = narrowed(n, fields)

    def row_of(n, k, r):
        return jnp.broadcast_to(constants[n, k, pl.ds(r, 1), :], (8, LANES))

    def level_coefs(n):
        if n == 0:
            tiles = [
                lambda k, t=t: jnp.broadcast_to(sides[t, k, pl.ds(gz, 1), :], (8, LANES))
                for t in range(2)
            ]
            tiles.append(
                lambda k: jnp.where(
                    lane < 64,
                    row_of(0, k, lax.rem(2 * gz + 2, 8)),
                    row_of(0, k, lax.rem(2 * gz + 7, 8)),
                )
            )
        elif n == 1:
            tiles = [
                lambda k: row_of(1, k, gz),
                lambda k: jnp.where(
                    lane < 64,
                    row_of(1, k, lax.rem(gz + 1, 4)),
                    row_of(1, k, lax.rem(gz + 3, 4)),
                ),
            ]
        elif n == 2:

            def one(k):
                here, there = row_of(2, k, gz // 2), row_of(2, k, 1 - gz // 2)
                lower = jnp.where(lane < 96, here, there)
                upper = pltpu.roll(jnp.where(lane < 32, there, here), 64, 1)
                return jnp.where(lax.rem(gz, 2) == 0, lower, upper)

            tiles = [one]
        else:
            tiles = [lambda k: row_of(3, k, 0)]
        return [[tile(k) for k in range(5)] for tile in tiles]

    def write_smoothed(g, carry):
        at, rows = pl.ds(XO + 4 * g, 4), pl.ds(YO, 64)
        moved = permuted(ping0[0, at, rows, :], ping0[1, at, rows, :], back[...])
        sm[pl.ds(4 * g, 4)] = moved.reshape(4, 64, 256)
        return carry

    for n, level in enumerate(LEVELS):
        raw, ext, packed, received, halved = raws[n], exts[n], packs[n], receiveds[n], halveds[n]
        if n > 0:
            pack_faces(level, raw, packed)
            copies = {}
            order = sorted(offsets_of(level), key=lambda o: -sum(abs(i) for i in o))
            for offset in order:
                copies[offset] = remote(
                    *message(level, raw, packed, ext, received, offset), offset
                )
                copies[offset].start()
            pending += list(copies.values())
        ping, pong = pings[n], pongs[n]
        if n == 1:
            coarser_constants()
        coefs = level_coefs(n)
        if n == 0:
            for offset, c in copies.items():
                if offset[0] == 0:
                    c.wait_recv()
            begin(level, raw, received, ext, coefs, ("own",))
            relax(level, ext, ping, pong, coefs, 0)
            for offset, c in copies.items():
                if offset[0] != 0:
                    c.wait_recv()
            begin(level, raw, received, ext, coefs, ("halo",))
            relax_wings(level, ext, ping, pong, coefs)
        else:
            if n == 1:
                lax.fori_loop(0, 4, write_smoothed, 0)
                stores = [pltpu.make_async_copy(sm, smooth_ref, local.at[2])]
                stores[0].start()
            for c in copies.values():
                c.wait_recv()
            begin(level, raw, received, ext, coefs, ("own", "halo"))
            relax(level, ext, ping, pong, coefs, HALO)
        residual_rows(level, ext, pings[n], coefs, pair, halved)
        if n == 1:
            raw2[0] = select_dot(halved[0].reshape(64, LANES), halving(0, 1.0)).reshape(
                4, 16, LANES
            )
        elif n == 2:
            k = lax.broadcasted_iota(jnp.int32, (LANES, LANES), 0)
            picks = jnp.where(k < 64, halving(32 * gz, 1.0), 0.0)
            column[gz] = select_dot(halved[0].reshape(16, LANES), picks).reshape(2, 8, LANES)

    copies = [remote(column.at[gz], column.at[gz], offset) for offset in PROFILE_PEERS]
    for c in copies:
        c.start()
    pending += copies
    coefs = level_coefs(3)
    for c in copies:
        c.wait_recv()
    whole = (column[0] + column[1]) + (column[2] + column[3])
    slab[...] = whole
    strip = pl.ds(pl.multiple_of(8 + 8 * gy, 8), 8)
    copies = [
        remote(slab, ext3.at[0, pl.ds(8 - 2 * offset[0], 2), strip, :], offset)
        for offset in COLUMN_PEERS
    ]
    for c in copies:
        c.start()
    ext3[0, pl.ds(8, 2), strip, :] = whole
    for c in pending:
        c.wait_send()
    for c in copies:
        c.wait_recv()

    def wrapped(target, x, values):
        for j in range(6):
            target[0, x, pl.ds(8 * j, 8), :] = values[(j - 1) % 4]

    ext3[0, 16] = ext3[0, 0]

    def start_all(x, carry):
        wrapped(ext3, x, [ext3[0, x, pl.ds(8 + 8 * j, 8), :] * coefs[0][3] for j in range(4)])
        return carry

    lax.fori_loop(1, 17, start_all, 0)

    sweeps(1, ext3, ping3, pong3, 1, 17, COARSE_SWEEPS - 1, 0, 4, coefs, wrapped)
    coarse_ref[...] = ping3[0, pl.ds(8, 2), pl.ds(8, 32), :]
    for c in copies:
        c.wait_send()
    stores[0].wait()


def hand_out(smoothed, coarse, smooth_out, coarse_out, sems):
    copies = [
        pltpu.make_async_copy(smoothed, smooth_out, sems.at[0]),
        pltpu.make_async_copy(coarse, coarse_out, sems.at[1]),
    ]
    for c in copies:
        c.start()
    for c in copies:
        c.wait()


def on_device(source, cell, face):
    f32 = jnp.float32
    messages = sum(len(offsets_of(level)) for level in LEVELS) + 6 + len(COLUMN_PEERS)
    vmem = pl.BlockSpec(memory_space=pltpu.VMEM)
    hbm = pl.BlockSpec(memory_space=pltpu.HBM)
    tile = (8, LANES)
    smoothed, coarse = pl.pallas_call(
        kernel,
        out_shape=(
            jax.ShapeDtypeStruct((16, 64, 256), f32),
            jax.ShapeDtypeStruct((2, 32, 128), f32),
        ),
        in_specs=[hbm, hbm, hbm],
        out_specs=(hbm, vmem),
        scratch_shapes=[
            pltpu.VMEM((2, 16, 64, LANES), f32),
            pltpu.VMEM((1, 8, 32, LANES), f32),
            pltpu.VMEM((1, 4, 16, LANES), f32),
            pltpu.VMEM(LEVELS[0]["shape"], f32),
            pltpu.VMEM(LEVELS[1]["shape"], f32),
            pltpu.VMEM(LEVELS[2]["shape"], f32),
            pltpu.VMEM((1, 18, 48, LANES), f32),
            pltpu.VMEM((2, 16, 64, LANES), f32),
            pltpu.VMEM((16, 64, 256), f32),
            pltpu.VMEM((256, 256), jnp.bfloat16),
            pltpu.VMEM((256, 256), jnp.bfloat16),
            pltpu.VMEM(LEVELS[0]["shape"], f32),
            pltpu.VMEM(LEVELS[1]["shape"], f32),
            pltpu.VMEM(LEVELS[2]["shape"], f32),
            pltpu.VMEM((1, 18, 48, LANES), f32),
            pltpu.VMEM(LEVELS[0]["shape"], f32),
            pltpu.VMEM(LEVELS[1]["shape"], f32),
            pltpu.VMEM(LEVELS[2]["shape"], f32),
            pltpu.VMEM((1, 18, 48, LANES), f32),
            pltpu.VMEM((2, 8) + tile, f32),
            pltpu.VMEM((1, 4) + tile, f32),
            pltpu.VMEM((1, 2) + tile, f32),
            pltpu.VMEM((2, 4, 10) + tile, f32),
            pltpu.VMEM((2, 3, 6) + tile, f32),
            pltpu.VMEM((2, 5, 4) + tile, f32),
            pltpu.VMEM((2, 256), f32),
            pltpu.VMEM((4,) + tile, f32),
            pltpu.VMEM((2,) + tile, f32),
            pltpu.VMEM((3, 2, 16, LANES), f32),
            pltpu.VMEM((4, 5) + tile, f32),
            pltpu.VMEM((2, 5) + tile, f32),
            pltpu.VMEM((64, LANES), f32),
            pltpu.VMEM((1, 4, 16, LANES), f32),
            pltpu.VMEM((1, 2, 8, LANES), f32),
            pltpu.VMEM((4, 2) + tile, f32),
            pltpu.VMEM((2,) + tile, f32),
            pltpu.SemaphoreType.DMA((messages,)),
            pltpu.SemaphoreType.DMA((messages,)),
            pltpu.SemaphoreType.DMA((6,)),
            pltpu.SemaphoreType.REGULAR((2,)),
        ],
        compiler_params=pltpu.CompilerParams(
            collective_id=0, has_side_effects=True, vmem_limit_bytes=52 << 20
        ),
    )(source, cell, face)
    return smoothed, coarse


def solution(mesh):
    return jax.shard_map(
        on_device,
        mesh=mesh,
        in_specs=(P("gx", "gy", "gz"), P("gz"), P("gz")),
        out_specs=(P("gx", "gy", "gz"), P("gx", None, None)),
        check_vma=False,
    )
```

```python
import jax
import jax.numpy as jnp
from jax import lax
from jax.experimental import pallas as pl
from jax.experimental.pallas import tpu as pltpu
from jax.sharding import PartitionSpec as P

MESH = pl.DeviceIdType.MESH
AXES = ("gx", "gy", "gz")
COUNTS = (8, 4, 4)
SWEEPS = 6
COARSE_SWEEPS = 8
HALO = 6
XO = 8
YO = 16
LANES = 128
DAMPING = 0.8

LEVELS = (
    dict(x=16, y=64, own=2, split=True, tiles=3, block=8, reach=1, step=1, shape=(3, 32, 96, LANES)),
    dict(x=8, y=32, own=1, split=False, tiles=2, block=8, reach=1, step=2, shape=(2, 24, 64, LANES)),
    dict(x=4, y=16, own=1, split=False, tiles=1, block=4, reach=2, step=0, shape=(1, 20, 48, LANES)),
)


def coordinates():
    return tuple(lax.axis_index(a) for a in AXES)


def device_at(place, offset):
    return tuple(
        lax.rem(p + (o + n), n) if o else p for p, o, n in zip(place, offset, COUNTS)
    )


def offsets_of(level):
    reach = level["reach"]
    return [
        (dx, dy, dz)
        for dx in range(-reach, reach + 1)
        for dy in (-1, 0, 1)
        for dz in (-1, 0, 1)
        if (dx, dy, dz) != (0, 0, 0)
    ]


FACES = ((1, 0, 0), (-1, 0, 0), (0, 1, 0), (0, -1, 0), (0, 0, 1), (0, 0, -1))
PROFILE_PEERS = ((0, 0, 1), (0, 0, -1), (0, 0, 2))
COLUMN_PEERS = tuple(
    (dx, dy, 0) for dx in (4, 3, -3, 2, -2, 1, -1, 0) for dy in (2, 1, -1, 0) if (dx, dy) != (0, 0)
)


def lane_iota(rows=8):
    return lax.broadcasted_iota(jnp.int32, (rows, LANES), 1)


def select_dot(rows, picks):
    return jnp.dot(
        rows, picks, preferred_element_type=jnp.float32, precision=lax.Precision.HIGHEST
    )


def as_bf16(hit):
    return jnp.where(hit, jnp.float32(1.0), jnp.float32(0.0)).astype(jnp.bfloat16)


def permuted(first, second, picks):
    rows = first.size // LANES
    left = jnp.concatenate([first.reshape(rows, LANES), second.reshape(rows, LANES)], axis=1)
    total = None
    for _ in range(3):
        term = left.astype(jnp.bfloat16)
        left = left - term.astype(jnp.float32)
        part = jnp.dot(term, picks, preferred_element_type=jnp.float32)
        total = part if total is None else total + part
    return total


def halving(shift, value, parity=None):
    k = lax.broadcasted_iota(jnp.int32, (LANES, LANES), 0)
    l = 2 * (lax.broadcasted_iota(jnp.int32, (LANES, LANES), 1) - shift)
    if parity is None:
        hit = (k == l) | (k == l + 1)
    else:
        hit = k == l + parity
    return jnp.where(hit, jnp.float32(value), jnp.float32(0.0))


def message(level, raw, packed, ext, received, offset):
    dx, dy, dz = offset
    nx, ny, own = level["x"], level["y"], level["own"]
    if dz == 0:
        if dx == 0:
            sx, tx, width = 0, XO, nx
        elif dx > 0:
            width = min(nx, HALO - (dx - 1) * nx)
            sx, tx = nx - width, XO - (dx - 1) * nx - width
        else:
            width = min(nx, HALO - (-dx - 1) * nx)
            sx, tx = 0, XO + nx + (-dx - 1) * nx
        if dy == 0:
            sy, ty, rows = 0, YO, ny
        elif dy > 0:
            sy, ty, rows = ny - 8, YO - 8, 8
        else:
            sy, ty, rows = 0, YO + ny, 8
        return (
            raw.at[pl.ds(0, own), pl.ds(sx, width), pl.ds(sy, rows), :],
            ext.at[pl.ds(0, own), pl.ds(tx, width), pl.ds(ty, rows), :],
        )
    blocks, strips, reach = nx // level["block"], ny // 8, level["reach"]
    if dx == 0:
        sb, tb, nb = 0, reach, blocks
    elif dx > 0:
        sb, tb, nb = blocks - 1, reach - dx, 1
    else:
        sb, tb, nb = 0, reach + blocks - 1 - dx, 1
    if dy == 0:
        ss, ts, ns = 0, 1, strips
    elif dy > 0:
        ss, ts, ns = strips - 1, 0, 1
    else:
        ss, ts, ns = 0, strips + 1, 1
    return (
        packed.at[pl.ds(sb, nb), pl.ds(ss, ns), :, :],
        received.at[0 if dz > 0 else 1, pl.ds(tb, nb), pl.ds(ts, ns), :, :],
    )


def pack_faces(level, raw, packed):
    lane = lane_iota()
    group = lane // 8
    own, block, strips = level["own"], level["block"], level["y"] // 8
    far = 15 if level["tiles"] > 1 else 7

    def strip(s, carry):
        rows = pl.ds(pl.multiple_of(8 * s, 8), 8)
        for b in range(level["x"] // block):
            total = jnp.zeros((8, LANES), jnp.float32)
            for i in range(block):
                ends = raw[0, b * block + i, rows, :]
                if own == 2:
                    ends = jnp.where(lane < 64, ends, raw[1, b * block + i, rows, :])
                moved = pltpu.roll(ends, 16 * i, 1) if i else ends
                mine = (group == 2 * i) | (group == (2 * i + far) % 16)
                total = jnp.where(mine, moved, total)
            packed[b, s] = total
        return carry

    lax.fori_loop(0, strips, strip, 0)


def vertical(level_tiles, wanted, centre):
    lane = lane_iota()

    def up(v):
        return pltpu.roll(v, 1, 1)

    def down(v):
        return pltpu.roll(v, LANES - 1, 1)

    if level_tiles == 1:
        return [(up(centre[0]), down(centre[0]))]
    if level_tiles == 2:
        ups, downs = [up(v) for v in centre], [down(v) for v in centre]
        return [
            (
                jnp.where(lane == 0, ups[1 - t], ups[t]),
                jnp.where(lane == LANES - 1, downs[1 - t], downs[t]),
            )
            for t in range(wanted)
        ]
    even, odd, halo = centre
    up_odd, down_even, up_halo, down_halo = up(odd), down(even), up(halo), down(halo)
    return [
        (jnp.where(lane == 0, up_halo, up_odd), odd),
        (even, jnp.where(lane == LANES - 1, down_halo, down_even)),
        (
            jnp.where(lane == 0, up_odd, up_halo),
            jnp.where(lane == LANES - 1, down_even, down_halo),
        ),
    ][:wanted]


def stencil(level_tiles, wanted, ext, x, row, coefs):
    centre = [ext[t, x, pl.ds(row, 8), :] for t in range(level_tiles)]
    sums = []
    for t, (beneath, overhead) in enumerate(vertical(level_tiles, wanted, centre)):
        around = (
            ext[t, x - 1, pl.ds(row, 8), :] + ext[t, x + 1, pl.ds(row, 8), :]
        ) + (ext[t, x, pl.ds(row - 1, 8), :] + ext[t, x, pl.ds(row + 1, 8), :])
        c, low, high, _, _ = coefs[t]
        sums.append(c * around + (low * beneath + high * overhead))
    return centre, sums


def update(tiles, beta, source, target, first, last, step, strips, coefs, finish):
    def planes(start):
        done = []
        for k in range(step):
            x = start + k
            values = []
            for j in range(strips):
                row = 8 + 8 * j
                centre, sums = stencil(tiles, tiles, source, x, row, coefs)
                for t in range(tiles):
                    if source is beta:
                        values.append(1.2 * centre[t] + sums[t])
                    else:
                        values.append((0.2 * centre[t] + beta[t, x, pl.ds(row, 8), :]) + sums[t])
            done.append((x, values))
        for x, values in done:
            finish(target, x, values)

    for_each(first, last, step, planes)


def for_each(first, last, step, body):
    if isinstance(first, int) and last - first == step:
        body(first)
        return

    def turn(i, carry):
        body(first + step * i)
        return carry

    lax.fori_loop(0, (last - first) // step, turn, 0)


def sweeps(tiles, beta, ping, pong, first, last, count, step, strips, coefs, finish):
    if step == 0:
        source = beta
        for s in range(1, count + 1):
            target = ping if s % 2 else pong
            lo, hi = first + s, last - s
            update(tiles, beta, source, target, lo, hi, hi - lo, strips, coefs, finish)
            source = target
        return
    update(tiles, beta, beta, ping, first + 1, last - 1, step, strips, coefs, finish)

    def two(k, carry):
        s = 2 * k + 2
        update(tiles, beta, ping, pong, first + s, last - s, step, strips, coefs, finish)
        update(tiles, beta, pong, ping, first + s + 1, last - s - 1, step, strips, coefs, finish)
        return carry

    lax.fori_loop(0, (count - 1) // 2, two, 0)


def finisher(level):
    tiles, strips = level["tiles"], level["y"] // 8 + 2

    def finish(target, x, values):
        for j in range(strips):
            for t in range(tiles):
                target[t, x, pl.ds(8 + 8 * j, 8), :] = values[j * tiles + t]

    return finish


def relax(level, ext, ping, pong, coefs, reach):
    sweeps(
        level["tiles"],
        ext,
        ping,
        pong,
        XO - reach,
        XO + level["x"] + reach,
        SWEEPS - 1,
        level["step"],
        level["y"] // 8 + 2,
        coefs,
        finisher(level),
    )


def relax_wings(level, ext, ping, pong, coefs):
    tiles, nx, strips = level["tiles"], level["x"], level["y"] // 8 + 2
    finish = finisher(level)

    def both(s, source, target):
        for first in (XO - HALO + s, XO + nx - s):
            update(tiles, ext, source, target, first, first + HALO, 1, strips, coefs, finish)

    both(1, ext, ping)

    def two(k, carry):
        both(2 * k + 2, ping, pong)
        both(2 * k + 3, pong, ping)
        return carry

    lax.fori_loop(0, (SWEEPS - 2) // 2, two, 0)


def begin(level, raw, received, ext, coefs, parts):
    tiles, own, nx, block = level["tiles"], level["own"], level["x"], level["block"]
    strips, blocks = level["y"] // 8 + 2, nx // block
    lane = lane_iota()
    even = lax.rem(lane // 8, 2) == 0
    base = 64 if tiles == 1 else 0

    def planes_of(e, planes, inside):
        for j in range(strips):
            row = 8 + 8 * j
            both = jnp.where(even, received[1, e, j], received[0, e, j])
            for i in planes:
                x = e * block + i
                shift = (base + LANES - 16 * i) % LANES
                ends = pltpu.roll(both, shift, 1) if shift else both
                for t in range(own):
                    if inside and 0 < j < strips - 1:
                        b = raw[t, x - XO, pl.ds(8 * (j - 1), 8), :]
                    else:
                        b = ext[t, x, pl.ds(row, 8), :]
                    if tiles == 1:
                        b = jnp.where(lane < 64, b, ends)
                    ext[t, x, pl.ds(row, 8), :] = b * coefs[t][3]
                if tiles > 1:
                    ext[own, x, pl.ds(row, 8), :] = ends * coefs[own][3]

    first = XO // block
    if "own" in parts:
        if blocks == 1:
            planes_of(first, range(block), True)
        else:

            def turn(e, carry):
                planes_of(e, range(block), True)
                return carry

            lax.fori_loop(first, first + blocks, turn, 0)
    if "halo" in parts:
        for e in list(range(first)) + list(range(first + blocks, first + blocks + XO // block)):
            planes = [i for i in range(block) if XO - HALO <= e * block + i < XO + nx + HALO]
            planes_of(e, planes, False)


def residual_rows(level, ext, ping, coefs, pair, halved):
    tiles, own, nx, ny = level["tiles"], level["own"], level["x"], level["y"]

    def planes(p):
        for j in range(ny // 8):
            row = YO + 8 * j
            total = [None] * own
            for k in range(2):
                x = XO + 2 * p + k
                centre, sums = stencil(tiles, own, ping, x, row, coefs)
                for t in range(own):
                    beta = ext[t, x, pl.ds(row, 8), :]
                    r = (beta - 0.8 * centre[t]) + sums[t]
                    total[t] = r if k == 0 else total[t] + r
            row_sum = total[0] * coefs[0][4]
            if own == 2:
                row_sum = row_sum + total[1] * coefs[1][4]
            pair[p, pl.ds(8 * j, 8), :] = row_sum

    def rows(p):
        halved[0, p] = 0.5 * (
            pair[p, pl.ds(0, ny // 2, stride=2), :] + pair[p, pl.ds(1, ny // 2, stride=2), :]
        )

    for body in (planes, rows):
        if own == 2:
            for_each(0, nx // 2, 1, body)
        else:
            for p in range(nx // 2):
                body(p)


def kernel(
    source_ref,
    cell_ref,
    face_ref,
    smooth_ref,
    coarse_ref,
    raw0,
    raw1,
    raw2,
    ext0,
    ext1,
    ext2,
    ext3,
    natural,
    sm,
    order,
    back,
    ping0,
    ping1,
    ping2,
    ping3,
    pong0,
    pong1,
    pong2,
    pong3,
    packed0,
    packed1,
    packed2,
    received0,
    received1,
    received2,
    line,
    profile,
    tables,
    spread,
    constants,
    sides,
    pair,
    halved1,
    halved2,
    column,
    slab,
    send,
    recv,
    local,
    greet,
):
    place = coordinates()
    gx, gy, gz = place
    counter = [0]

    def remote(source, target, offset):
        k = counter[0]
        counter[0] += 1
        return pltpu.make_async_remote_copy(
            src_ref=source,
            dst_ref=target,
            send_sem=send.at[k],
            recv_sem=recv.at[k],
            device_id=device_at(place, offset),
            device_id_type=MESH,
        )

    pings, pongs = (ping0, ping1, ping2), (pong0, pong1, pong2)
    raws, exts = (raw0, raw1, raw2), (ext0, ext1, ext2)
    packs, receiveds = (packed0, packed1, packed2), (received0, received1, received2)
    halveds = (raw1, halved1, halved2)

    barrier = pltpu.get_barrier_semaphore()
    peers = FACES + ((0, 0, 2), (0, 1, 1), (0, 1, -1), (0, -1, 1), (0, -1, -1))
    for offset in peers:
        pl.semaphore_signal(
            barrier, inc=1, device_id=device_at(place, offset), device_id_type=MESH
        )
    loads = [
        pltpu.make_async_copy(
            source_ref.at[:, :, pl.ds(LANES * t, LANES)], natural.at[t], local.at[t]
        )
        for t in range(2)
    ]
    loads.append(pltpu.make_async_copy(cell_ref, line.at[0], local.at[4]))
    loads.append(pltpu.make_async_copy(face_ref, line.at[1], local.at[5]))
    for c in loads:
        c.start()
    mine = profile.at[gz]
    for c in loads:
        c.wait()
    for t in range(2):
        profile[gz, pl.ds(t, 1), :] = line[0, pl.ds(LANES * t, LANES)].reshape(1, LANES)
        profile[gz, pl.ds(2 + t, 1), :] = line[1, pl.ds(LANES * t, LANES)].reshape(1, LANES)
    z_from = lax.broadcasted_iota(jnp.int32, (256, 256), 0)
    z_to = lax.broadcasted_iota(jnp.int32, (256, 256), 1)
    order[...] = as_bf16(z_from == 2 * lax.rem(z_to, LANES) + z_to // LANES)
    back[...] = as_bf16(z_to == 2 * lax.rem(z_from, LANES) + z_from // LANES)

    def sort_cells(g, carry):
        at = pl.ds(4 * g, 4)
        moved = permuted(natural[0, at], natural[1, at], order[...])
        raw0[0, at] = moved[:, :LANES].reshape(4, 64, LANES)
        raw0[1, at] = moved[:, LANES:].reshape(4, 64, LANES)
        return carry

    lax.fori_loop(0, 4, sort_cells, 0)
    pack_faces(LEVELS[0], natural, packed0)
    pl.semaphore_wait(barrier, len(peers))

    pending = []
    copies = {}
    for offset in offsets_of(LEVELS[0]):
        copies[offset] = remote(
            *message(LEVELS[0], raw0, packed0, ext0, received0, offset), offset
        )
    profiles = [remote(mine, mine, offset) for offset in PROFILE_PEERS]
    for c in profiles:
        c.start()
    for offset in peers[:1:-1]:
        if offset in copies:
            copies[offset].start()
    for stage, distance in ((0, 2), (1, 3)):
        for offset in FACES:
            pl.semaphore_signal(
                greet.at[stage], inc=1, device_id=device_at(place, offset), device_id_type=MESH
            )
        pl.semaphore_wait(greet.at[stage], len(FACES))
        for offset in sorted(copies, key=lambda o: abs(o[0])):
            if offset in peers[2:]:
                continue
            if sum(abs(o) for o in offset) == distance:
                copies[offset].start()
            elif distance == 2 and offset in FACES[:2]:
                copies[offset].start()
    pending += list(copies.values()) + profiles

    for c in profiles:
        c.wait_recv()
    lane = lane_iota()
    row = lax.broadcasted_iota(jnp.int32, (8, LANES), 0)
    for z in range(4):
        for t in range(2):
            tables[0, pl.ds(2 * z + t, 1), :] = profile[z, pl.ds(t, 1), :]
            tables[1, pl.ds(2 * z + t, 1), :] = profile[z, pl.ds(2 + t, 1), :]
    cell, below = tables[0], tables[1]
    turned = pltpu.roll(below, LANES - 1, 1)
    above = jnp.where(lane == LANES - 1, pltpu.roll(turned, 7, 0), turned)
    above = jnp.where((row == 7) & (lane == LANES - 1), 0.0, above)
    first, second = halving(0, 1.0, 0), halving(0, 1.0, 1)
    first, second = first + halving(64, 1.0, 0), second + halving(64, 1.0, 1)
    picks = jnp.concatenate([first, second], axis=1)

    def keep(ref, cell, below, above, bottom):
        diag = 4.0 * cell + below + above
        scale = DAMPING / diag
        ref[0] = cell * scale
        ref[1] = jnp.where((row == 0) & (lane == 0), 0.0, below * scale) if bottom else below * scale
        ref[2] = above * scale
        ref[3] = scale
        ref[4] = diag * (1.0 / DAMPING)

    def narrowed(n, fields):
        halves = []
        for k, values in enumerate(fields):
            taken = select_dot(values, picks)
            for p in range(2):
                spread[k, p, pl.ds(0, 8), :] = taken[:, LANES * p : LANES * (p + 1)]
        for k in range(3):
            halves.append(
                [
                    jnp.where(
                        row < 8 >> (n + 1),
                        jnp.where(
                            lane < 64,
                            spread[k, p, pl.ds(0, 8, stride=2), :],
                            spread[k, p, pl.ds(1, 8, stride=2), :],
                        ),
                        1.0,
                    )
                    for p in range(2)
                ]
            )
        return halves

    keep(constants.at[0], cell, below, above, True)
    finest = narrowed(0, (cell, below, above))
    for p in range(2):
        keep(sides.at[p], *[field[p] for field in finest], p == 0)

    def coarser_constants():
        halves = finest
        for n in range(1, 4):
            cells, belows, aboves = halves
            fields = (0.5 * (cells[0] + cells[1]), belows[0], aboves[1])
            keep(constants.at[n], *fields, True)
            if n < 3:
                halves = narrowed(n, fields)

    def row_of(n, k, r):
        return jnp.broadcast_to(constants[n, k, pl.ds(r, 1), :], (8, LANES))

    def level_coefs(n):
        if n == 0:
            tiles = [
                lambda k, t=t: jnp.broadcast_to(sides[t, k, pl.ds(gz, 1), :], (8, LANES))
                for t in range(2)
            ]
            tiles.append(
                lambda k: jnp.where(
                    lane < 64,
                    row_of(0, k, lax.rem(2 * gz + 2, 8)),
                    row_of(0, k, lax.rem(2 * gz + 7, 8)),
                )
            )
        elif n == 1:
            tiles = [
                lambda k: row_of(1, k, gz),
                lambda k: jnp.where(
                    lane < 64,
                    row_of(1, k, lax.rem(gz + 1, 4)),
                    row_of(1, k, lax.rem(gz + 3, 4)),
                ),
            ]
        elif n == 2:

            def one(k):
                here, there = row_of(2, k, gz // 2), row_of(2, k, 1 - gz // 2)
                lower = jnp.where(lane < 96, here, there)
                upper = pltpu.roll(jnp.where(lane < 32, there, here), 64, 1)
                return jnp.where(lax.rem(gz, 2) == 0, lower, upper)

            tiles = [one]
        else:
            tiles = [lambda k: row_of(3, k, 0)]
        return [[tile(k) for k in range(5)] for tile in tiles]

    def write_smoothed(g, carry):
        at, rows = pl.ds(XO + 4 * g, 4), pl.ds(YO, 64)
        moved = permuted(ping0[0, at, rows, :], ping0[1, at, rows, :], back[...])
        sm[pl.ds(4 * g, 4)] = moved.reshape(4, 64, 256)
        return carry

    for n, level in enumerate(LEVELS):
        raw, ext, packed, received, halved = raws[n], exts[n], packs[n], receiveds[n], halveds[n]
        if n > 0:
            pack_faces(level, raw, packed)
            copies = {}
            order = sorted(offsets_of(level), key=lambda o: (abs(o[2])==0, -sum(abs(i) for i in o)))
            for offset in order:
                copies[offset] = remote(
                    *message(level, raw, packed, ext, received, offset), offset
                )
                copies[offset].start()
            pending += list(copies.values())
        ping, pong = pings[n], pongs[n]
        if n == 1:
            coarser_constants()
        coefs = level_coefs(n)
        if n == 0:
            for offset, c in copies.items():
                if offset[0] == 0:
                    c.wait_recv()
            begin(level, raw, received, ext, coefs, ("own",))
            relax(level, ext, ping, pong, coefs, 0)
            for offset, c in copies.items():
                if offset[0] != 0:
                    c.wait_recv()
            begin(level, raw, received, ext, coefs, ("halo",))
            relax_wings(level, ext, ping, pong, coefs)
        else:
            if n == 1:
                lax.fori_loop(0, 4, write_smoothed, 0)
                stores = [pltpu.make_async_copy(sm, smooth_ref, local.at[2])]
                stores[0].start()
            for c in copies.values():
                c.wait_recv()
            begin(level, raw, received, ext, coefs, ("own", "halo"))
            relax(level, ext, ping, pong, coefs, HALO)
        residual_rows(level, ext, pings[n], coefs, pair, halved)
        if n == 1:
            raw2[0] = select_dot(halved[0].reshape(64, LANES), halving(0, 1.0)).reshape(
                4, 16, LANES
            )
        elif n == 2:
            k = lax.broadcasted_iota(jnp.int32, (LANES, LANES), 0)
            picks = jnp.where(k < 64, halving(32 * gz, 1.0), 0.0)
            column[gz] = select_dot(halved[0].reshape(16, LANES), picks).reshape(2, 8, LANES)

    copies = [remote(column.at[gz], column.at[gz], offset) for offset in PROFILE_PEERS]
    for c in copies:
        c.start()
    pending += copies
    coefs = level_coefs(3)
    for c in copies:
        c.wait_recv()
    whole = (column[0] + column[1]) + (column[2] + column[3])
    slab[...] = whole
    strip = pl.ds(pl.multiple_of(8 + 8 * gy, 8), 8)
    copies = [
        remote(slab, ext3.at[0, pl.ds(8 - 2 * offset[0], 2), strip, :], offset)
        for offset in COLUMN_PEERS
    ]
    for c in copies:
        c.start()
    ext3[0, pl.ds(8, 2), strip, :] = whole
    for c in pending:
        c.wait_send()
    for c in copies:
        c.wait_recv()

    def wrapped(target, x, values):
        for j in range(6):
            target[0, x, pl.ds(8 * j, 8), :] = values[(j - 1) % 4]

    ext3[0, 16] = ext3[0, 0]

    def start_all(x, carry):
        wrapped(ext3, x, [ext3[0, x, pl.ds(8 + 8 * j, 8), :] * coefs[0][3] for j in range(4)])
        return carry

    lax.fori_loop(1, 17, start_all, 0)

    sweeps(1, ext3, ping3, pong3, 1, 17, COARSE_SWEEPS - 1, 0, 4, coefs, wrapped)
    coarse_ref[...] = ping3[0, pl.ds(8, 2), pl.ds(8, 32), :]
    for c in copies:
        c.wait_send()
    stores[0].wait()


def hand_out(smoothed, coarse, smooth_out, coarse_out, sems):
    copies = [
        pltpu.make_async_copy(smoothed, smooth_out, sems.at[0]),
        pltpu.make_async_copy(coarse, coarse_out, sems.at[1]),
    ]
    for c in copies:
        c.start()
    for c in copies:
        c.wait()


def on_device(source, cell, face):
    f32 = jnp.float32
    messages = sum(len(offsets_of(level)) for level in LEVELS) + 6 + len(COLUMN_PEERS)
    vmem = pl.BlockSpec(memory_space=pltpu.VMEM)
    hbm = pl.BlockSpec(memory_space=pltpu.HBM)
    tile = (8, LANES)
    smoothed, coarse = pl.pallas_call(
        kernel,
        out_shape=(
            jax.ShapeDtypeStruct((16, 64, 256), f32),
            jax.ShapeDtypeStruct((2, 32, 128), f32),
        ),
        in_specs=[hbm, hbm, hbm],
        out_specs=(hbm, vmem),
        scratch_shapes=[
            pltpu.VMEM((2, 16, 64, LANES), f32),
            pltpu.VMEM((1, 8, 32, LANES), f32),
            pltpu.VMEM((1, 4, 16, LANES), f32),
            pltpu.VMEM(LEVELS[0]["shape"], f32),
            pltpu.VMEM(LEVELS[1]["shape"], f32),
            pltpu.VMEM(LEVELS[2]["shape"], f32),
            pltpu.VMEM((1, 18, 48, LANES), f32),
            pltpu.VMEM((2, 16, 64, LANES), f32),
            pltpu.VMEM((16, 64, 256), f32),
            pltpu.VMEM((256, 256), jnp.bfloat16),
            pltpu.VMEM((256, 256), jnp.bfloat16),
            pltpu.VMEM(LEVELS[0]["shape"], f32),
            pltpu.VMEM(LEVELS[1]["shape"], f32),
            pltpu.VMEM(LEVELS[2]["shape"], f32),
            pltpu.VMEM((1, 18, 48, LANES), f32),
            pltpu.VMEM(LEVELS[0]["shape"], f32),
            pltpu.VMEM(LEVELS[1]["shape"], f32),
            pltpu.VMEM(LEVELS[2]["shape"], f32),
            pltpu.VMEM((1, 18, 48, LANES), f32),
            pltpu.VMEM((2, 8) + tile, f32),
            pltpu.VMEM((1, 4) + tile, f32),
            pltpu.VMEM((1, 2) + tile, f32),
            pltpu.VMEM((2, 4, 10) + tile, f32),
            pltpu.VMEM((2, 3, 6) + tile, f32),
            pltpu.VMEM((2, 5, 4) + tile, f32),
            pltpu.VMEM((2, 256), f32),
            pltpu.VMEM((4,) + tile, f32),
            pltpu.VMEM((2,) + tile, f32),
            pltpu.VMEM((3, 2, 16, LANES), f32),
            pltpu.VMEM((4, 5) + tile, f32),
            pltpu.VMEM((2, 5) + tile, f32),
            pltpu.VMEM((8, 64, LANES), f32),
            pltpu.VMEM((1, 4, 16, LANES), f32),
            pltpu.VMEM((1, 2, 8, LANES), f32),
            pltpu.VMEM((4, 2) + tile, f32),
            pltpu.VMEM((2,) + tile, f32),
            pltpu.SemaphoreType.DMA((messages,)),
            pltpu.SemaphoreType.DMA((messages,)),
            pltpu.SemaphoreType.DMA((6,)),
            pltpu.SemaphoreType.REGULAR((2,)),
        ],
        compiler_params=pltpu.CompilerParams(
            collective_id=0, has_side_effects=True, vmem_limit_bytes=52 << 20
        ),
    )(source, cell, face)
    return smoothed, coarse


def solution(mesh):
    return jax.shard_map(
        on_device,
        mesh=mesh,
        in_specs=(P("gx", "gy", "gz"), P("gz"), P("gz")),
        out_specs=(P("gx", "gy", "gz"), P("gx", None, None)),
        check_vma=False,
    )
```

```python
import jax
import jax.numpy as jnp
from jax import lax
from jax.experimental import pallas as pl
from jax.experimental.pallas import tpu as pltpu
from jax.sharding import PartitionSpec as P

MESH = pl.DeviceIdType.MESH
AXES = ("gx", "gy", "gz")
COUNTS = (8, 4, 4)
SWEEPS = 6
COARSE_SWEEPS = 8
HALO = 6
XO = 8
YO = 16
LANES = 128
DAMPING = 0.8

LEVELS = (
    dict(x=16, y=64, own=2, split=True, tiles=3, block=8, reach=1, step=1, shape=(3, 32, 96, LANES)),
    dict(x=8, y=32, own=1, split=False, tiles=2, block=8, reach=1, step=0, shape=(2, 24, 64, LANES)),
    dict(x=4, y=16, own=1, split=False, tiles=1, block=4, reach=2, step=0, shape=(1, 20, 48, LANES)),
)


def coordinates():
    return tuple(lax.axis_index(a) for a in AXES)


def device_at(place, offset):
    return tuple(
        lax.rem(p + (o + n), n) if o else p for p, o, n in zip(place, offset, COUNTS)
    )


def offsets_of(level):
    reach = level["reach"]
    return [
        (dx, dy, dz)
        for dx in range(-reach, reach + 1)
        for dy in (-1, 0, 1)
        for dz in (-1, 0, 1)
        if (dx, dy, dz) != (0, 0, 0)
    ]


FACES = ((1, 0, 0), (-1, 0, 0), (0, 1, 0), (0, -1, 0), (0, 0, 1), (0, 0, -1))
PROFILE_PEERS = ((0, 0, 1), (0, 0, -1), (0, 0, 2))
COLUMN_PEERS = tuple(
    (dx, dy, 0) for dx in (4, 3, -3, 2, -2, 1, -1, 0) for dy in (2, 1, -1, 0) if (dx, dy) != (0, 0)
)


def lane_iota(rows=8):
    return lax.broadcasted_iota(jnp.int32, (rows, LANES), 1)


def select_dot(rows, picks):
    return jnp.dot(
        rows, picks, preferred_element_type=jnp.float32, precision=lax.Precision.HIGHEST
    )


def as_bf16(hit):
    return jnp.where(hit, jnp.float32(1.0), jnp.float32(0.0)).astype(jnp.bfloat16)


def permuted(first, second, picks):
    rows = first.size // LANES
    left = jnp.concatenate([first.reshape(rows, LANES), second.reshape(rows, LANES)], axis=1)
    total = None
    for _ in range(3):
        term = left.astype(jnp.bfloat16)
        left = left - term.astype(jnp.float32)
        part = jnp.dot(term, picks, preferred_element_type=jnp.float32)
        total = part if total is None else total + part
    return total


def halving(shift, value, parity=None):
    k = lax.broadcasted_iota(jnp.int32, (LANES, LANES), 0)
    l = 2 * (lax.broadcasted_iota(jnp.int32, (LANES, LANES), 1) - shift)
    if parity is None:
        hit = (k == l) | (k == l + 1)
    else:
        hit = k == l + parity
    return jnp.where(hit, jnp.float32(value), jnp.float32(0.0))


def message(level, raw, packed, ext, received, offset):
    dx, dy, dz = offset
    nx, ny, own = level["x"], level["y"], level["own"]
    if dz == 0:
        if dx == 0:
            sx, tx, width = 0, XO, nx
        elif dx > 0:
            width = min(nx, HALO - (dx - 1) * nx)
            sx, tx = nx - width, XO - (dx - 1) * nx - width
        else:
            width = min(nx, HALO - (-dx - 1) * nx)
            sx, tx = 0, XO + nx + (-dx - 1) * nx
        if dy == 0:
            sy, ty, rows = 0, YO, ny
        elif dy > 0:
            sy, ty, rows = ny - 8, YO - 8, 8
        else:
            sy, ty, rows = 0, YO + ny, 8
        return (
            raw.at[pl.ds(0, own), pl.ds(sx, width), pl.ds(sy, rows), :],
            ext.at[pl.ds(0, own), pl.ds(tx, width), pl.ds(ty, rows), :],
        )
    blocks, strips, reach = nx // level["block"], ny // 8, level["reach"]
    if dx == 0:
        sb, tb, nb = 0, reach, blocks
    elif dx > 0:
        sb, tb, nb = blocks - 1, reach - dx, 1
    else:
        sb, tb, nb = 0, reach + blocks - 1 - dx, 1
    if dy == 0:
        ss, ts, ns = 0, 1, strips
    elif dy > 0:
        ss, ts, ns = strips - 1, 0, 1
    else:
        ss, ts, ns = 0, strips + 1, 1
    return (
        packed.at[pl.ds(sb, nb), pl.ds(ss, ns), :, :],
        received.at[0 if dz > 0 else 1, pl.ds(tb, nb), pl.ds(ts, ns), :, :],
    )


def pack_faces(level, raw, packed):
    lane = lane_iota()
    group = lane // 8
    own, block, strips = level["own"], level["block"], level["y"] // 8
    far = 15 if level["tiles"] > 1 else 7

    def strip(s, carry):
        rows = pl.ds(pl.multiple_of(8 * s, 8), 8)
        for b in range(level["x"] // block):
            total = jnp.zeros((8, LANES), jnp.float32)
            for i in range(block):
                ends = raw[0, b * block + i, rows, :]
                if own == 2:
                    ends = jnp.where(lane < 64, ends, raw[1, b * block + i, rows, :])
                moved = pltpu.roll(ends, 16 * i, 1) if i else ends
                mine = (group == 2 * i) | (group == (2 * i + far) % 16)
                total = jnp.where(mine, moved, total)
            packed[b, s] = total
        return carry

    lax.fori_loop(0, strips, strip, 0)


def vertical(level_tiles, wanted, centre):
    lane = lane_iota()

    def up(v):
        return pltpu.roll(v, 1, 1)

    def down(v):
        return pltpu.roll(v, LANES - 1, 1)

    if level_tiles == 1:
        return [(up(centre[0]), down(centre[0]))]
    if level_tiles == 2:
        ups, downs = [up(v) for v in centre], [down(v) for v in centre]
        return [
            (
                jnp.where(lane == 0, ups[1 - t], ups[t]),
                jnp.where(lane == LANES - 1, downs[1 - t], downs[t]),
            )
            for t in range(wanted)
        ]
    even, odd, halo = centre
    up_odd, down_even, up_halo, down_halo = up(odd), down(even), up(halo), down(halo)
    return [
        (jnp.where(lane == 0, up_halo, up_odd), odd),
        (even, jnp.where(lane == LANES - 1, down_halo, down_even)),
        (
            jnp.where(lane == 0, up_odd, up_halo),
            jnp.where(lane == LANES - 1, down_even, down_halo),
        ),
    ][:wanted]


def stencil(level_tiles, wanted, ext, x, row, coefs):
    centre = [ext[t, x, pl.ds(row, 8), :] for t in range(level_tiles)]
    sums = []
    for t, (beneath, overhead) in enumerate(vertical(level_tiles, wanted, centre)):
        around = (
            ext[t, x - 1, pl.ds(row, 8), :] + ext[t, x + 1, pl.ds(row, 8), :]
        ) + (ext[t, x, pl.ds(row - 1, 8), :] + ext[t, x, pl.ds(row + 1, 8), :])
        c, low, high, _, _ = coefs[t]
        sums.append(c * around + (low * beneath + high * overhead))
    return centre, sums


def update(tiles, beta, source, target, first, last, step, strips, coefs, finish):
    def planes(start):
        done = []
        for k in range(step):
            x = start + k
            values = []
            for j in range(strips):
                row = 8 + 8 * j
                centre, sums = stencil(tiles, tiles, source, x, row, coefs)
                for t in range(tiles):
                    if source is beta:
                        values.append(1.2 * centre[t] + sums[t])
                    else:
                        values.append((0.2 * centre[t] + beta[t, x, pl.ds(row, 8), :]) + sums[t])
            done.append((x, values))
        for x, values in done:
            finish(target, x, values)

    for_each(first, last, step, planes)


def for_each(first, last, step, body):
    if isinstance(first, int) and last - first == step:
        body(first)
        return

    def turn(i, carry):
        body(first + step * i)
        return carry

    lax.fori_loop(0, (last - first) // step, turn, 0)


def sweeps(tiles, beta, ping, pong, first, last, count, step, strips, coefs, finish):
    if step == 0:
        source = beta
        for s in range(1, count + 1):
            target = ping if s % 2 else pong
            lo, hi = first + s, last - s
            update(tiles, beta, source, target, lo, hi, hi - lo, strips, coefs, finish)
            source = target
        return
    update(tiles, beta, beta, ping, first + 1, last - 1, step, strips, coefs, finish)

    def two(k, carry):
        s = 2 * k + 2
        update(tiles, beta, ping, pong, first + s, last - s, step, strips, coefs, finish)
        update(tiles, beta, pong, ping, first + s + 1, last - s - 1, step, strips, coefs, finish)
        return carry

    lax.fori_loop(0, (count - 1) // 2, two, 0)


def finisher(level):
    tiles, strips = level["tiles"], level["y"] // 8 + 2

    def finish(target, x, values):
        for j in range(strips):
            for t in range(tiles):
                target[t, x, pl.ds(8 + 8 * j, 8), :] = values[j * tiles + t]

    return finish


def relax(level, ext, ping, pong, coefs, reach):
    sweeps(
        level["tiles"],
        ext,
        ping,
        pong,
        XO - reach,
        XO + level["x"] + reach,
        SWEEPS - 1,
        level["step"],
        level["y"] // 8 + 2,
        coefs,
        finisher(level),
    )


def relax_wings(level, ext, ping, pong, coefs):
    tiles, nx, strips = level["tiles"], level["x"], level["y"] // 8 + 2
    finish = finisher(level)

    def both(s, source, target):
        for first in (XO - HALO + s, XO + nx - s):
            update(tiles, ext, source, target, first, first + HALO, 3, strips, coefs, finish)

    both(1, ext, ping)

    def two(k, carry):
        both(2 * k + 2, ping, pong)
        both(2 * k + 3, pong, ping)
        return carry

    lax.fori_loop(0, (SWEEPS - 2) // 2, two, 0)


def begin(level, raw, received, ext, coefs, parts):
    tiles, own, nx, block = level["tiles"], level["own"], level["x"], level["block"]
    strips, blocks = level["y"] // 8 + 2, nx // block
    lane = lane_iota()
    even = lax.rem(lane // 8, 2) == 0
    base = 64 if tiles == 1 else 0

    def planes_of(e, planes, inside):
        for j in range(strips):
            row = 8 + 8 * j
            both = jnp.where(even, received[1, e, j], received[0, e, j])
            for i in planes:
                x = e * block + i
                shift = (base + LANES - 16 * i) % LANES
                ends = pltpu.roll(both, shift, 1) if shift else both
                for t in range(own):
                    if inside and 0 < j < strips - 1:
                        b = raw[t, x - XO, pl.ds(8 * (j - 1), 8), :]
                    else:
                        b = ext[t, x, pl.ds(row, 8), :]
                    if tiles == 1:
                        b = jnp.where(lane < 64, b, ends)
                    ext[t, x, pl.ds(row, 8), :] = b * coefs[t][3]
                if tiles > 1:
                    ext[own, x, pl.ds(row, 8), :] = ends * coefs[own][3]

    first = XO // block
    if "own" in parts:
        if blocks == 1:
            planes_of(first, range(block), True)
        else:

            def turn(e, carry):
                planes_of(e, range(block), True)
                return carry

            lax.fori_loop(first, first + blocks, turn, 0)
    if "halo" in parts:
        for e in list(range(first)) + list(range(first + blocks, first + blocks + XO // block)):
            planes = [i for i in range(block) if XO - HALO <= e * block + i < XO + nx + HALO]
            planes_of(e, planes, False)


def residual_rows(level, ext, ping, coefs, pair, halved):
    tiles, own, nx, ny = level["tiles"], level["own"], level["x"], level["y"]

    def planes(p):
        for j in range(ny // 8):
            row = YO + 8 * j
            total = [None] * own
            for k in range(2):
                x = XO + 2 * p + k
                centre, sums = stencil(tiles, own, ping, x, row, coefs)
                for t in range(own):
                    beta = ext[t, x, pl.ds(row, 8), :]
                    r = (beta - 0.8 * centre[t]) + sums[t]
                    total[t] = r if k == 0 else total[t] + r
            row_sum = total[0] * coefs[0][4]
            if own == 2:
                row_sum = row_sum + total[1] * coefs[1][4]
            pair[p, pl.ds(8 * j, 8), :] = row_sum

    def rows(p):
        halved[0, p] = 0.5 * (
            pair[p, pl.ds(0, ny // 2, stride=2), :] + pair[p, pl.ds(1, ny // 2, stride=2), :]
        )

    for body in (planes, rows):
        if own == 2:
            for_each(0, nx // 2, 1, body)
        else:
            for p in range(nx // 2):
                body(p)


def kernel(
    source_ref,
    cell_ref,
    face_ref,
    smooth_ref,
    coarse_ref,
    raw0,
    raw1,
    raw2,
    ext0,
    ext1,
    ext2,
    ext3,
    natural,
    sm,
    order,
    back,
    ping0,
    ping1,
    ping2,
    ping3,
    pong0,
    pong1,
    pong2,
    pong3,
    packed0,
    packed1,
    packed2,
    received0,
    received1,
    received2,
    line,
    profile,
    tables,
    spread,
    constants,
    sides,
    pair,
    halved1,
    halved2,
    column,
    slab,
    send,
    recv,
    local,
    greet,
):
    place = coordinates()
    gx, gy, gz = place
    counter = [0]

    def remote(source, target, offset):
        k = counter[0]
        counter[0] += 1
        return pltpu.make_async_remote_copy(
            src_ref=source,
            dst_ref=target,
            send_sem=send.at[k],
            recv_sem=recv.at[k],
            device_id=device_at(place, offset),
            device_id_type=MESH,
        )

    pings, pongs = (ping0, ping1, ping2), (pong0, pong1, pong2)
    raws, exts = (raw0, raw1, raw2), (ext0, ext1, ext2)
    packs, receiveds = (packed0, packed1, packed2), (received0, received1, received2)
    halveds = (raw1, halved1, halved2)

    barrier = pltpu.get_barrier_semaphore()
    peers = FACES + ((0, 0, 2), (0, 1, 1), (0, 1, -1), (0, -1, 1), (0, -1, -1))
    for offset in peers:
        pl.semaphore_signal(
            barrier, inc=1, device_id=device_at(place, offset), device_id_type=MESH
        )
    loads = [
        pltpu.make_async_copy(
            source_ref.at[:, :, pl.ds(LANES * t, LANES)], natural.at[t], local.at[t]
        )
        for t in range(2)
    ]
    loads.append(pltpu.make_async_copy(cell_ref, line.at[0], local.at[4]))
    loads.append(pltpu.make_async_copy(face_ref, line.at[1], local.at[5]))
    for c in loads:
        c.start()
    mine = profile.at[gz]
    for c in loads:
        c.wait()
    for t in range(2):
        profile[gz, pl.ds(t, 1), :] = line[0, pl.ds(LANES * t, LANES)].reshape(1, LANES)
        profile[gz, pl.ds(2 + t, 1), :] = line[1, pl.ds(LANES * t, LANES)].reshape(1, LANES)
    z_from = lax.broadcasted_iota(jnp.int32, (256, 256), 0)
    z_to = lax.broadcasted_iota(jnp.int32, (256, 256), 1)
    order[...] = as_bf16(z_from == 2 * lax.rem(z_to, LANES) + z_to // LANES)
    back[...] = as_bf16(z_to == 2 * lax.rem(z_from, LANES) + z_from // LANES)

    def sort_cells(g, carry):
        at = pl.ds(4 * g, 4)
        moved = permuted(natural[0, at], natural[1, at], order[...])
        raw0[0, at] = moved[:, :LANES].reshape(4, 64, LANES)
        raw0[1, at] = moved[:, LANES:].reshape(4, 64, LANES)
        return carry

    lax.fori_loop(0, 4, sort_cells, 0)
    pack_faces(LEVELS[0], natural, packed0)
    pl.semaphore_wait(barrier, len(peers))

    pending = []
    copies = {}
    for offset in offsets_of(LEVELS[0]):
        copies[offset] = remote(
            *message(LEVELS[0], raw0, packed0, ext0, received0, offset), offset
        )
    profiles = [remote(mine, mine, offset) for offset in PROFILE_PEERS]
    for c in profiles:
        c.start()
    for offset in peers[:1:-1]:
        if offset in copies:
            copies[offset].start()
    for stage, distance in ((0, 2), (1, 3)):
        for offset in FACES:
            pl.semaphore_signal(
                greet.at[stage], inc=1, device_id=device_at(place, offset), device_id_type=MESH
            )
        pl.semaphore_wait(greet.at[stage], len(FACES))
        for offset in sorted(copies, key=lambda o: abs(o[0])):
            if offset in peers[2:]:
                continue
            if sum(abs(o) for o in offset) == distance:
                copies[offset].start()
            elif distance == 2 and offset in FACES[:2]:
                copies[offset].start()
    pending += list(copies.values()) + profiles

    for c in profiles:
        c.wait_recv()
    lane = lane_iota()
    row = lax.broadcasted_iota(jnp.int32, (8, LANES), 0)
    for z in range(4):
        for t in range(2):
            tables[0, pl.ds(2 * z + t, 1), :] = profile[z, pl.ds(t, 1), :]
            tables[1, pl.ds(2 * z + t, 1), :] = profile[z, pl.ds(2 + t, 1), :]
    cell, below = tables[0], tables[1]
    turned = pltpu.roll(below, LANES - 1, 1)
    above = jnp.where(lane == LANES - 1, pltpu.roll(turned, 7, 0), turned)
    above = jnp.where((row == 7) & (lane == LANES - 1), 0.0, above)
    first, second = halving(0, 1.0, 0), halving(0, 1.0, 1)
    first, second = first + halving(64, 1.0, 0), second + halving(64, 1.0, 1)
    picks = jnp.concatenate([first, second], axis=1)

    def keep(ref, cell, below, above, bottom):
        diag = 4.0 * cell + below + above
        scale = DAMPING / diag
        ref[0] = cell * scale
        ref[1] = jnp.where((row == 0) & (lane == 0), 0.0, below * scale) if bottom else below * scale
        ref[2] = above * scale
        ref[3] = scale
        ref[4] = diag * (1.0 / DAMPING)

    def narrowed(n, fields):
        halves = []
        for k, values in enumerate(fields):
            taken = select_dot(values, picks)
            for p in range(2):
                spread[k, p, pl.ds(0, 8), :] = taken[:, LANES * p : LANES * (p + 1)]
        for k in range(3):
            halves.append(
                [
                    jnp.where(
                        row < 8 >> (n + 1),
                        jnp.where(
                            lane < 64,
                            spread[k, p, pl.ds(0, 8, stride=2), :],
                            spread[k, p, pl.ds(1, 8, stride=2), :],
                        ),
                        1.0,
                    )
                    for p in range(2)
                ]
            )
        return halves

    keep(constants.at[0], cell, below, above, True)
    finest = narrowed(0, (cell, below, above))
    for p in range(2):
        keep(sides.at[p], *[field[p] for field in finest], p == 0)

    def coarser_constants():
        halves = finest
        for n in range(1, 4):
            cells, belows, aboves = halves
            fields = (0.5 * (cells[0] + cells[1]), belows[0], aboves[1])
            keep(constants.at[n], *fields, True)
            if n < 3:
                halves = narrowed(n, fields)

    def row_of(n, k, r):
        return jnp.broadcast_to(constants[n, k, pl.ds(r, 1), :], (8, LANES))

    def level_coefs(n):
        if n == 0:
            tiles = [
                lambda k, t=t: jnp.broadcast_to(sides[t, k, pl.ds(gz, 1), :], (8, LANES))
                for t in range(2)
            ]
            tiles.append(
                lambda k: jnp.where(
                    lane < 64,
                    row_of(0, k, lax.rem(2 * gz + 2, 8)),
                    row_of(0, k, lax.rem(2 * gz + 7, 8)),
                )
            )
        elif n == 1:
            tiles = [
                lambda k: row_of(1, k, gz),
                lambda k: jnp.where(
                    lane < 64,
                    row_of(1, k, lax.rem(gz + 1, 4)),
                    row_of(1, k, lax.rem(gz + 3, 4)),
                ),
            ]
        elif n == 2:

            def one(k):
                here, there = row_of(2, k, gz // 2), row_of(2, k, 1 - gz // 2)
                lower = jnp.where(lane < 96, here, there)
                upper = pltpu.roll(jnp.where(lane < 32, there, here), 64, 1)
                return jnp.where(lax.rem(gz, 2) == 0, lower, upper)

            tiles = [one]
        else:
            tiles = [lambda k: row_of(3, k, 0)]
        return [[tile(k) for k in range(5)] for tile in tiles]

    def write_smoothed(g, carry):
        at, rows = pl.ds(XO + 4 * g, 4), pl.ds(YO, 64)
        moved = permuted(ping0[0, at, rows, :], ping0[1, at, rows, :], back[...])
        sm[pl.ds(4 * g, 4)] = moved.reshape(4, 64, 256)
        return carry

    for n, level in enumerate(LEVELS):
        raw, ext, packed, received, halved = raws[n], exts[n], packs[n], receiveds[n], halveds[n]
        if n > 0:
            pack_faces(level, raw, packed)
            copies = {}
            order = sorted(offsets_of(level), key=lambda o: (abs(o[2])==0, -sum(abs(i) for i in o)))
            for offset in order:
                copies[offset] = remote(
                    *message(level, raw, packed, ext, received, offset), offset
                )
                copies[offset].start()
            pending += list(copies.values())
        ping, pong = pings[n], pongs[n]
        if n == 1:
            coarser_constants()
        coefs = level_coefs(n)
        if n == 0:
            for offset, c in copies.items():
                if offset[0] == 0:
                    c.wait_recv()
            begin(level, raw, received, ext, coefs, ("own",))
            relax(level, ext, ping, pong, coefs, 0)
            for offset, c in copies.items():
                if offset[0] != 0:
                    c.wait_recv()
            begin(level, raw, received, ext, coefs, ("halo",))
            relax_wings(level, ext, ping, pong, coefs)
        else:
            if n == 1:
                lax.fori_loop(0, 4, write_smoothed, 0)
                stores = [pltpu.make_async_copy(sm, smooth_ref, local.at[2])]
                stores[0].start()
            for c in copies.values():
                c.wait_recv()
            begin(level, raw, received, ext, coefs, ("own", "halo"))
            relax(level, ext, ping, pong, coefs, HALO)
        residual_rows(level, ext, pings[n], coefs, pair, halved)
        if n == 1:
            raw2[0] = select_dot(halved[0].reshape(64, LANES), halving(0, 1.0)).reshape(
                4, 16, LANES
            )
        elif n == 2:
            k = lax.broadcasted_iota(jnp.int32, (LANES, LANES), 0)
            picks = jnp.where(k < 64, halving(32 * gz, 1.0), 0.0)
            column[gz] = select_dot(halved[0].reshape(16, LANES), picks).reshape(2, 8, LANES)

    copies = [remote(column.at[gz], column.at[gz], offset) for offset in PROFILE_PEERS]
    for c in copies:
        c.start()
    pending += copies
    coefs = level_coefs(3)
    for c in copies:
        c.wait_recv()
    whole = (column[0] + column[1]) + (column[2] + column[3])
    slab[...] = whole
    strip = pl.ds(pl.multiple_of(8 + 8 * gy, 8), 8)
    copies = [
        remote(slab, ext3.at[0, pl.ds(8 - 2 * offset[0], 2), strip, :], offset)
        for offset in COLUMN_PEERS
    ]
    for c in copies:
        c.start()
    ext3[0, pl.ds(8, 2), strip, :] = whole
    for c in pending:
        c.wait_send()
    for c in copies:
        c.wait_recv()

    def wrapped(target, x, values):
        for j in range(6):
            target[0, x, pl.ds(8 * j, 8), :] = values[(j - 1) % 4]

    ext3[0, 16] = ext3[0, 0]

    def start_all(x, carry):
        wrapped(ext3, x, [ext3[0, x, pl.ds(8 + 8 * j, 8), :] * coefs[0][3] for j in range(4)])
        return carry

    lax.fori_loop(1, 17, start_all, 0)

    sweeps(1, ext3, ping3, pong3, 1, 17, COARSE_SWEEPS - 1, 0, 4, coefs, wrapped)
    coarse_ref[...] = ping3[0, pl.ds(8, 2), pl.ds(8, 32), :]
    for c in copies:
        c.wait_send()
    stores[0].wait()


def hand_out(smoothed, coarse, smooth_out, coarse_out, sems):
    copies = [
        pltpu.make_async_copy(smoothed, smooth_out, sems.at[0]),
        pltpu.make_async_copy(coarse, coarse_out, sems.at[1]),
    ]
    for c in copies:
        c.start()
    for c in copies:
        c.wait()


def on_device(source, cell, face):
    f32 = jnp.float32
    messages = sum(len(offsets_of(level)) for level in LEVELS) + 6 + len(COLUMN_PEERS)
    vmem = pl.BlockSpec(memory_space=pltpu.VMEM)
    hbm = pl.BlockSpec(memory_space=pltpu.HBM)
    tile = (8, LANES)
    smoothed, coarse = pl.pallas_call(
        kernel,
        out_shape=(
            jax.ShapeDtypeStruct((16, 64, 256), f32),
            jax.ShapeDtypeStruct((2, 32, 128), f32),
        ),
        in_specs=[hbm, hbm, hbm],
        out_specs=(hbm, vmem),
        scratch_shapes=[
            pltpu.VMEM((2, 16, 64, LANES), f32),
            pltpu.VMEM((1, 8, 32, LANES), f32),
            pltpu.VMEM((1, 4, 16, LANES), f32),
            pltpu.VMEM(LEVELS[0]["shape"], f32),
            pltpu.VMEM(LEVELS[1]["shape"], f32),
            pltpu.VMEM(LEVELS[2]["shape"], f32),
            pltpu.VMEM((1, 18, 48, LANES), f32),
            pltpu.VMEM((2, 16, 64, LANES), f32),
            pltpu.VMEM((16, 64, 256), f32),
            pltpu.VMEM((256, 256), jnp.bfloat16),
            pltpu.VMEM((256, 256), jnp.bfloat16),
            pltpu.VMEM(LEVELS[0]["shape"], f32),
            pltpu.VMEM(LEVELS[1]["shape"], f32),
            pltpu.VMEM(LEVELS[2]["shape"], f32),
            pltpu.VMEM((1, 18, 48, LANES), f32),
            pltpu.VMEM(LEVELS[0]["shape"], f32),
            pltpu.VMEM(LEVELS[1]["shape"], f32),
            pltpu.VMEM(LEVELS[2]["shape"], f32),
            pltpu.VMEM((1, 18, 48, LANES), f32),
            pltpu.VMEM((2, 8) + tile, f32),
            pltpu.VMEM((1, 4) + tile, f32),
            pltpu.VMEM((1, 2) + tile, f32),
            pltpu.VMEM((2, 4, 10) + tile, f32),
            pltpu.VMEM((2, 3, 6) + tile, f32),
            pltpu.VMEM((2, 5, 4) + tile, f32),
            pltpu.VMEM((2, 256), f32),
            pltpu.VMEM((4,) + tile, f32),
            pltpu.VMEM((2,) + tile, f32),
            pltpu.VMEM((3, 2, 16, LANES), f32),
            pltpu.VMEM((4, 5) + tile, f32),
            pltpu.VMEM((2, 5) + tile, f32),
            pltpu.VMEM((8, 64, LANES), f32),
            pltpu.VMEM((1, 4, 16, LANES), f32),
            pltpu.VMEM((1, 2, 8, LANES), f32),
            pltpu.VMEM((4, 2) + tile, f32),
            pltpu.VMEM((2,) + tile, f32),
            pltpu.SemaphoreType.DMA((messages,)),
            pltpu.SemaphoreType.DMA((messages,)),
            pltpu.SemaphoreType.DMA((6,)),
            pltpu.SemaphoreType.REGULAR((2,)),
        ],
        compiler_params=pltpu.CompilerParams(
            collective_id=0, has_side_effects=True, vmem_limit_bytes=52 << 20
        ),
    )(source, cell, face)
    return smoothed, coarse


def solution(mesh):
    return jax.shard_map(
        on_device,
        mesh=mesh,
        in_specs=(P("gx", "gy", "gz"), P("gz"), P("gz")),
        out_specs=(P("gx", "gy", "gz"), P("gx", None, None)),
        check_vma=False,
    )
```
